128 devices in a mesh: orow: 16 (over z, x), ocol: 8 (over y, core).
Axes of the slice: x: 4, y: 4, z: 4, core: 2. Of those that a mesh axis runs over, the one named last changes fastest.
Arguments:
- integrals: bfloat16 [2304, 32, 384], P('ocol', 'orow'), may hold values from -0.29882812 to 0.29882812
- occ_count: int32 [16], replicated, may hold values from 1 to 2
- occ_energy: float32 [32], replicated, may hold values from -2 to -0.5
- vir_energy: float32 [384], replicated, may hold values from 0.3 to 2.5
- task_iblock: int32 [64, 1], replicated, may hold values from 0 to 15; in each aligned block of 64 rows (0 to 63, 64 to 127, ...) at most 8 rows name the same one
- task_jblock: int32 [64], replicated, may hold values from 0 to 15
Outputs:
- gamma_out: float32 [2304, 32, 384], P('ocol', 'orow')
- density: float32 [384, 384], replicated
The draws below stay inside these ranges and needn't reach their ends.
Inputs may be any that keep to these rules, and one draw needn't show every extreme that they name: `task_iblock`: no first block is named by more than 8 tasks, and some first block by exactly 8.
All inputs are finite; a program needn't handle non-finite values.
Results may differ from the reference program's by a relative error of at most 0.0019.
Values may be sent and summed in bfloat16 or wider, within the bound.
No kernel may reach another device: no remote copies, remote signals or barrier semaphores. Data moves between devices by JAX's collectives and lax.ppermute only.
A program may use at most 128 MiB of HBM per device.

```python
import math
import jax
import jax.numpy as jnp
import numpy as np
from jax import lax

NAUX = 2304
NVIR = 384
OB = 2
MOST = 8
TASKS = 64
OCC = 32
N_OROW = 16


def with_ends(result, stream_key, least, largest):
    extent = result.shape
    index_at = [jax.random.randint(jax.random.fold_in(stream_key, axis), (), 0, extent[axis]) for axis in range(len(extent))]
    result = result.at[tuple(index_at)].set(least)
    longest = extent.index(max(extent))
    index_at[longest] = (index_at[longest] + 1) % extent[longest]
    return result.at[tuple(index_at)].set(largest)


def block_levels(rng, dims, shards, low, top_value):
    loudness = 1.0
    for position, parts in shards:
        heights = jax.random.uniform(jax.random.fold_in(jax.random.fold_in(rng, 6), position), (parts,), jnp.float32, low / len(shards), top_value / len(shards))
        loudness = loudness * jnp.repeat(jnp.exp(heights), dims[position] // parts).reshape((-1,) + (1,) * (len(dims) - 1 - position))
    return loudness


def deal_out(rng, own, number, rows, count, top, reach, skew):
    order = jax.random.permutation(rng, count)
    crowded, ordinary = shares(count, rows * top, reach, skew, True), shares(count, rows * top, reach, skew, False)
    places = jnp.arange(count)

    def named(tallies, turn):
        used = int((tallies > 0).sum())
        fixed = max(1, used // 4)
        shifted = fixed + (places - fixed + turn * (used - fixed)) % max(1, count - fixed)
        return jnp.zeros((count,), jnp.int32).at[order[jnp.where(places < fixed, places, shifted)]].set(jnp.asarray(tallies, jnp.int32))

    tallies = jnp.where(number % 4 == 0, named(crowded, number // 4), named(ordinary, number - number // 4 - 1))
    mixed = jax.random.permutation(jax.random.fold_in(own, 3), count)
    source_of, taker = mixed[0:count // 2 * 2:2], mixed[1:count // 2 * 2:2]
    slack = jnp.minimum(tallies[source_of] - 1, reach - tallies[taker]) // 2
    slack = jnp.where((source_of == order[0]) | (taker == order[0]) | (tallies[taker] == 0), 0, jnp.maximum(slack, 0))
    shifted = jax.random.randint(jax.random.fold_in(own, 4), (count // 2,), 0, 1 << 20) % (slack + 1)
    tallies = tallies.at[source_of].add(-shifted).at[taker].add(shifted)
    items = jnp.searchsorted(jnp.cumsum(tallies), jnp.arange(rows * top), side="right").astype(jnp.int32)
    table = items.reshape(top, rows).T
    table = table[jax.random.permutation(jax.random.fold_in(own, 1), rows)]
    turn = jax.random.randint(jax.random.fold_in(own, 2), (rows, 1), 0, top)
    return jnp.take_along_axis(table, (jnp.arange(top)[None, :] + turn) % top, axis=1)


def shares(amount, total, most, lean, full):
    portions = [(1 << 20) // math.isqrt(grade ** lean) + 1 for grade in range(1, amount + 1)]
    largest = most if full else min(most, max(-(-total // amount), total * portions[0] // sum(portions)))
    least = 1 if total - largest >= amount - 1 else 0
    given, surplus = [largest] + [least] * (amount - 1), total - largest - least * (amount - 1)
    while surplus > 0:
        movable = [i for i in range(1, amount) if given[i] < largest] or [i for i in range(1, amount) if given[i] < most]
        pool, left = sum([portions[i] for i in movable]), surplus
        for i in movable:
            more = min(most - given[i], max(1, left * portions[i] // pool), surplus)
            given[i] = given[i] + more
            surplus = surplus - more
    return np.array(given)


def centred(stream_key, dims, scale, bound, pieces=(), kind=jnp.bfloat16):
    result = scale * jax.random.normal(stream_key, dims, jnp.float32)
    if pieces:
        result = result * block_levels(stream_key, dims, pieces, -0.22, 0.18)
    return jnp.clip(result, -bound, bound).astype(kind)


def setup_inputs(seed: int = 0) -> dict:
    key_list = jax.random.split(jax.random.key(seed), 7)
    integrals = centred(key_list[0], (NAUX, OCC, NVIR), 0.05, 0.29882812, ((0, 8), (1, 16)))
    occ_count = with_ends(jax.random.randint(key_list[1], (N_OROW,), 1, OB + 1), jax.random.fold_in(key_list[1], 1), 1, OB).astype(jnp.int32)
    occ_energy = jnp.clip(jax.random.uniform(key_list[2], (OCC,), jnp.float32, -2.0, -0.5), -2.0, -0.5)
    vir_energy = jnp.clip(jax.random.uniform(key_list[3], (NVIR,), jnp.float32, 0.3, 2.5), 0.3, 2.5)
    task_iblock_keys = jax.random.split(jax.random.fold_in(key_list[4], 1), TASKS // TASKS)
    task_iblock_turns = jax.random.permutation(jax.random.fold_in(key_list[4], 3), TASKS // TASKS)
    task_iblock = jax.vmap(lambda own, number: deal_out(jax.random.fold_in(key_list[4], 2), own, number, TASKS, N_OROW, 1, MOST, 2))(task_iblock_keys, task_iblock_turns).reshape((TASKS, 1))
    task_jblock = with_ends(jax.random.randint(key_list[5], (TASKS,), 0, N_OROW), jax.random.fold_in(key_list[5], 1), 0, N_OROW - 1).astype(jnp.int32)
    return {"integrals": integrals, "occ_count": occ_count, "occ_energy": occ_energy, "vir_energy": vir_energy, "task_iblock": task_iblock, "task_jblock": task_jblock}


def amplitude(k_total, i_energy, j_energy, vir_energy):
    orbitals = i_energy.shape[0]
    virtuals = vir_energy.shape[0]
    k_grid = k_total.reshape(orbitals, virtuals, orbitals, virtuals)
    denominator = (i_energy[:, None, None, None] + j_energy[None, None, :, None]
                   - vir_energy[None, :, None, None] - vir_energy[None, None, None, :])
    values = (2.0 * k_grid - jnp.swapaxes(k_grid, 1, 3)) / denominator
    return values.reshape(orbitals * virtuals, orbitals * virtuals)


def reference(integrals, occ_count, occ_energy, vir_energy, task_iblock, task_jblock):
    orbital_ids = jnp.arange(OCC, dtype=jnp.int32)
    active = (orbital_ids % OB) < occ_count[orbital_ids // OB]
    masked = integrals * active.astype(jnp.bfloat16)[None, :, None]
    flat_blocks = masked.reshape(NAUX, N_OROW, OB * NVIR)
    energy_grid = occ_energy.reshape(N_OROW, OB)

    def step(carry, pair):
        gamma_sum, dens_sum = carry
        first, second = pair
        i_rows = lax.dynamic_index_in_dim(flat_blocks, first, 1, keepdims=False)
        j_rows = lax.dynamic_index_in_dim(flat_blocks, second, 1, keepdims=False)
        k_total = jnp.dot(i_rows.T, j_rows, preferred_element_type=jnp.float32)
        i_energy = lax.dynamic_index_in_dim(energy_grid, first, 0, keepdims=False)
        j_energy = lax.dynamic_index_in_dim(energy_grid, second, 0, keepdims=False)
        amplitudes = amplitude(k_total, i_energy, j_energy, vir_energy).astype(jnp.bfloat16)
        gamma_i = jnp.dot(j_rows, amplitudes.T, preferred_element_type=jnp.float32)
        gamma_j = jnp.dot(i_rows, amplitudes, preferred_element_type=jnp.float32)
        gamma_sum = gamma_sum.at[:, first].add(gamma_i).at[:, second].add(gamma_j)
        grid = amplitudes.astype(jnp.float32).reshape(OB, NVIR, OB * NVIR)
        dens_sum = dens_sum + jnp.einsum('iaw,ibw->ab', grid, grid)
        return (gamma_sum, dens_sum), None

    start = (jnp.zeros((NAUX, N_OROW, OB * NVIR), jnp.float32), jnp.zeros((NVIR, NVIR), jnp.float32))
    pairs = (task_iblock[:, 0].astype(jnp.int32), task_jblock.astype(jnp.int32))
    (gamma_sum, dens_sum), _ = lax.scan(step, start, pairs)
    gamma_out = gamma_sum.reshape(NAUX, OCC, NVIR)
    density = dens_sum / TASKS
    return gamma_out, density
```

```python
import functools

import jax
import jax.numpy as jnp
from jax import lax
from jax.experimental import pallas as pl
from jax.experimental.pallas import tpu as pltpu
from jax.sharding import Mesh
from jax.sharding import PartitionSpec as P

AXES = ("z", "x", "y", "c")
OROW = ("z", "x")
OCOL = ("y", "c")


def shift(axis, s):
    n = lax.axis_size(axis)
    return [(i, (i + s) % n) for i in range(n)]


def move(x, axis, s):
    return lax.ppermute(x, axis, shift(axis, s))


def swap(x, axis, bits):
    return lax.ppermute(x, axis, [(i, i ^ bits) for i in range(lax.axis_size(axis))])


def to_plane():
    pairs = []
    for z in range(4):
        for x in range(4):
            for y in range(4):
                for c in range(2):
                    source = ((z * 4 + x) * 4 + y) * 2 + c
                    target = ((y * 4 + 2 * (x // 2) + c) * 4 + z) * 2 + x % 2
                    pairs.append((source, target))
    return pairs


def amp_kernel(scal_ref, g_ref, r_ref, row_ref, col_ref, ampt_ref, dens_ref):
    j, i = pl.program_id(0), pl.program_id(1)
    left = r_ref[...].reshape(-1, r_ref.shape[-1])
    right = g_ref[...].reshape(-1, g_ref.shape[-1])
    k = lax.dot_general(
        left, right, (((0,), (0,)), ((), ())), preferred_element_type=jnp.float32
    )
    kt = k.T
    pair = scal_ref[i] + scal_ref[2 + j]
    delta = (pair - col_ref[...]) - row_ref[...]
    amp = ((2.0 * k - kt) / delta).astype(jnp.bfloat16)
    ampt = ((2.0 * kt - k) / delta).astype(jnp.bfloat16)
    ampt_ref[0, 0] = ampt
    part = scal_ref[6 + j // 2] * jnp.dot(amp, ampt, preferred_element_type=jnp.float32)

    @pl.when((j == 0) & (i == 0))
    def _():
        dens_ref[...] = part

    @pl.when((j != 0) | (i != 0))
    def _():
        dens_ref[...] += part


def gamma_kernel(scal_ref, g_ref, ampt_ref, out_ref):
    v = g_ref.shape[-1]
    for i in range(2):
        total = None
        for h in range(2):
            part = jnp.dot(
                g_ref[0, h, 0, 0], ampt_ref[2 * h, i], preferred_element_type=jnp.float32
            ) + jnp.dot(
                g_ref[0, h, 0, 1], ampt_ref[2 * h + 1, i], preferred_element_type=jnp.float32
            )
            part = part * scal_ref[8 + h]
            total = part if total is None else total + part
        out_ref[:, i * v : (i + 1) * v] = total


def local(integrals, occ_count, occ_energy, vir_energy, task_iblock, task_jblock):
    slice_rows, orbitals, virtuals = integrals.shape
    z, x, y, c = (lax.axis_index(a) for a in AXES)
    my_row = z * 4 + x
    active = jnp.arange(orbitals) < occ_count[my_row]
    masked = jnp.swapaxes(integrals * active.astype(jnp.bfloat16)[None, :, None], 0, 1)

    planed = lax.ppermute(masked, AXES, to_plane())
    right = lax.all_gather(planed, OROW)
    left = lax.all_gather(masked, OCOL)
    right = right.reshape(4, 2, 2, orbitals, slice_rows, virtuals)

    blocks = 4 * y + 2 * jnp.arange(2) + c
    first, second = task_iblock[:, 0], task_jblock
    ours = ((first == my_row)[:, None] & (second[:, None] == blocks[None])).sum(0)
    theirs = ((second == my_row)[:, None] & (first[:, None] == blocks[None])).sum(0)
    energy = occ_energy.reshape(-1, orbitals)
    scal = jnp.concatenate(
        [
            energy[my_row],
            energy[blocks].reshape(-1),
            ours.astype(jnp.float32),
            (ours + theirs).astype(jnp.float32),
        ]
    )

    smem = pl.BlockSpec(memory_space=pltpu.SMEM)
    ampt, dens = pl.pallas_call(
        amp_kernel,
        grid=(4, 2),
        in_specs=[
            smem,
            pl.BlockSpec(
                (4, 1, 2, 1, slice_rows, virtuals), lambda j, i: (0, j // 2, 0, j % 2, 0, 0)
            ),
            pl.BlockSpec((8, 1, slice_rows, virtuals), lambda j, i: (0, i, 0, 0)),
            pl.BlockSpec((1, virtuals), lambda j, i: (0, 0)),
            pl.BlockSpec((virtuals, 1), lambda j, i: (0, 0)),
        ],
        out_specs=[
            pl.BlockSpec((1, 1, virtuals, virtuals), lambda j, i: (j, i, 0, 0)),
            pl.BlockSpec((virtuals, virtuals), lambda j, i: (0, 0)),
        ],
        out_shape=[
            jax.ShapeDtypeStruct((4, 2, virtuals, virtuals), jnp.bfloat16),
            jax.ShapeDtypeStruct((virtuals, virtuals), jnp.float32),
        ],
        cost_estimate=pl.CostEstimate(
            flops=6_200_000_000, bytes_accessed=14_000_000, transcendentals=0
        ),
        name="amplitudes",
    )(scal, right, left, vir_energy.reshape(1, -1), vir_energy.reshape(-1, 1))

    gamma_parts = pl.pallas_call(
        gamma_kernel,
        grid=(8,),
        in_specs=[
            smem,
            pl.BlockSpec(
                (1, 2, 1, 2, slice_rows, virtuals), lambda s: (s // 2, 0, s % 2, 0, 0, 0)
            ),
            pl.BlockSpec((4, 2, virtuals, virtuals), lambda s: (0, 0, 0, 0)),
        ],
        out_specs=pl.BlockSpec((slice_rows, 2 * virtuals), lambda s: (s, 0)),
        out_shape=jax.ShapeDtypeStruct((8 * slice_rows, 2 * virtuals), jnp.float32),
        cost_estimate=pl.CostEstimate(
            flops=5_400_000_000, bytes_accessed=17_000_000, transcendentals=0
        ),
        name="gamma",
    )(scal, right, ampt)
    gamma = lax.psum_scatter(gamma_parts, OCOL, scatter_dimension=0, tiled=True)
    gamma_out = gamma.reshape(slice_rows, orbitals, virtuals)

    half = virtuals // 2
    halves = dens.reshape(2, half, virtuals)
    keep = lax.dynamic_index_in_dim(halves, c, 0, keepdims=False)
    give = lax.dynamic_index_in_dim(halves, 1 - c, 0, keepdims=False)
    part = (keep + swap(give, "c", 1)).reshape(4, half // 4, virtuals)
    piece = lambda s: lax.dynamic_index_in_dim(part, (y + s) % 4, 0, keepdims=False)
    own = piece(0) + move(piece(1), "y", 1) + move(piece(3), "y", 3) + move(piece(2), "y", 2)
    for axis in ("x", "z"):
        own = own + swap(own, axis, 1)
        own = own + swap(own, axis, 3)
    own = own / task_iblock.shape[0]
    around = jnp.stack([own] + [move(own, "y", s) for s in (1, 2, 3)])
    mine = around[(y - jnp.arange(4)) % 4].reshape(half, virtuals)
    other = swap(mine, "c", 1)
    density = jnp.where(c == 0, jnp.concatenate([mine, other]), jnp.concatenate([other, mine]))
    return gamma_out, density


def solution(mesh):
    finer = Mesh(mesh.devices.reshape(4, 4, 4, 2), AXES)
    placed = (P(OCOL, OROW, None), P(), P(), P(), P(), P())
    return jax.shard_map(
        local, mesh=finer, in_specs=placed, out_specs=(P(OCOL, OROW, None), P()), check_vma=False
    )
```

```python
import jax
import jax.numpy as jnp
from jax import lax
from jax.experimental import pallas as pl
from jax.experimental.pallas import tpu as pltpu
from jax.sharding import Mesh
from jax.sharding import PartitionSpec as P

AXES = ("z", "x", "y", "c")
OROW = ("z", "x")
OCOL = ("y", "c")
BF16 = jnp.bfloat16
F32 = jnp.float32
ANY = pl.BlockSpec(memory_space=pl.ANY)
SMEM = pl.BlockSpec(memory_space=pltpu.SMEM)


def move(x, axis, s):
    n = lax.axis_size(axis)
    return lax.ppermute(x, axis, [(i, (i + s) % n) for i in range(n)])


def swap(x):
    return lax.ppermute(x, "c", [(0, 1), (1, 0)])


def to_plane():
    pairs = []
    for z in range(4):
        for x in range(4):
            for y in range(4):
                for c in range(2):
                    source = ((z * 4 + x) * 4 + y) * 2 + c
                    target = (((2 * (z // 2) + c) * 4 + (x + y) % 4) * 4 + x) * 2 + z % 2
                    pairs.append((source, target))
    return pairs


def turn_kernel(slot_ref, *refs):
    pieces, out_ref, held, sem = refs[:8], refs[8], refs[9], refs[10]
    rows = pieces[0].shape[1]
    copies = [
        pltpu.make_async_copy(
            piece, held.at[:, pl.ds(pl.multiple_of(slot_ref[n] * rows, rows), rows), :], sem.at[n]
        )
        for n, piece in enumerate(pieces)
    ]
    for copy in copies:
        copy.start()
    for copy in copies:
        copy.wait()
    v = held.shape[2]
    for i in range(2):
        out_ref[i * v : (i + 1) * v, :] = held[i].T


def amp_kernel(place_ref, scal_ref, left_ref, row_ref, col_ref, *refs):
    sets_a, sets_b = refs[0:4], refs[4:8]
    ampt_ref, dens_ref, right_ref = refs[8:11]
    held, k_ref, amp_ref, sem, out_sem = refs[11:]
    rows, v = sets_a[0].shape[1:]

    def piece(source, slot, h, half):
        at = pl.ds(pl.multiple_of(slot * rows, rows), rows)
        return pltpu.make_async_copy(
            source, held.at[h, at, half * v : (half + 1) * v], sem.at[h]
        )

    for s in range(4):
        for t in range(4):
            for source, zs, xs, half in ((sets_a[s], s, t, 0), (sets_b[s], t, s, 1)):
                zz = place_ref[zs]
                piece(
                    source.at[t], 2 * place_ref[4 + xs] + lax.rem(zz, 2), zz // 2, half
                ).start()
    for h in range(2):
        for _ in range(16):
            piece(sets_a[0].at[0], 0, h, 0).wait()
        copy_out = pltpu.make_async_copy(held.at[h], right_ref.at[h], out_sem.at[h])
        copy_out.start()
        k_ref[...] = jnp.dot(left_ref[...], held[h], preferred_element_type=F32)
        for i in range(2):
            for j in range(2):
                a, b = slice(i * v, (i + 1) * v), slice(j * v, (j + 1) * v)
                k = k_ref[a, b]
                kt = k.T
                pair = scal_ref[i] + scal_ref[2 + 2 * h + j]
                delta = (pair - col_ref[...]) - row_ref[...]
                amp_ref[a, b] = ((2.0 * k - kt) / delta).astype(BF16)
                ampt_ref[h, b, a] = ((2.0 * kt - k) / delta).astype(BF16)
        part = None
        for i in range(2):
            a = slice(i * v, (i + 1) * v)
            prod = jnp.dot(amp_ref[a, :], ampt_ref[h, :, a], preferred_element_type=F32)
            part = prod if part is None else part + prod
        part = scal_ref[6 + h] * part
        if h == 0:
            dens_ref[...] = part
        else:
            dens_ref[...] += part
    for h in range(2):
        pltpu.make_async_copy(held.at[h], right_ref.at[h], out_sem.at[h]).wait()


def gamma_kernel(slot_ref, scal_ref, right_ref, ampt_ref, out_ref):
    total = scal_ref[8] * jnp.dot(right_ref[0], ampt_ref[0], preferred_element_type=F32)
    out_ref[0] = total + scal_ref[9] * jnp.dot(
        right_ref[1], ampt_ref[1], preferred_element_type=F32
    )


def four_sum(x, axis):
    return (x + move(x, axis, 2)) + (move(x, axis, 1) + move(x, axis, 3))


def local(integrals, occ_count, occ_energy, vir_energy, task_iblock, task_jblock):
    rows, orbitals, v = integrals.shape
    z, x, y, c = (lax.axis_index(a) for a in AXES)
    my_row = z * 4 + x
    steps = jnp.arange(4)
    active = jnp.arange(orbitals) < occ_count[my_row]
    masked = jnp.swapaxes(integrals * active.astype(BF16)[None, :, None], 0, 1)

    planed = lax.ppermute(masked, AXES, to_plane())
    around = [masked] + [move(masked, "y", s) for s in (1, 2, 3)]
    across = [swap(p) for p in around]
    first_a = jnp.stack([planed[0]] + [move(planed[0], "x", s) for s in (1, 2, 3)])
    first_b = jnp.stack([planed[1]] + [move(planed[1], "z", s) for s in (1, 2, 3)])
    sets_a = [first_a] + [move(first_a, "z", s) for s in (1, 2, 3)]
    sets_b = [first_b] + [move(first_b, "x", s) for s in (1, 2, 3)]

    ys = (y - steps) % 4
    slots = jnp.concatenate([2 * ys + c, 2 * ys + 1 - c]).astype(jnp.int32)
    place = jnp.concatenate([(z - steps) % 4, (x - steps - y) % 4]).astype(jnp.int32)
    blocks = 4 * (2 * jnp.arange(2) + c) + y
    first, second = task_iblock[:, 0], task_jblock
    ours = ((first == my_row)[:, None] & (second[:, None] == blocks[None])).sum(0)
    theirs = ((second == my_row)[:, None] & (first[:, None] == blocks[None])).sum(0)
    energy = occ_energy.reshape(-1, orbitals)
    scal = jnp.concatenate(
        [
            energy[my_row],
            energy[blocks].reshape(-1),
            ours.astype(F32),
            (ours + theirs).astype(F32),
        ]
    )

    left = pl.pallas_call(
        turn_kernel,
        in_specs=[SMEM] + [ANY] * 8,
        out_specs=pl.BlockSpec(memory_space=pltpu.VMEM),
        out_shape=jax.ShapeDtypeStruct((2 * v, 8 * rows), BF16),
        scratch_shapes=[pltpu.VMEM((2, 8 * rows, v), BF16), pltpu.SemaphoreType.DMA((8,))],
        cost_estimate=pl.CostEstimate(flops=0, bytes_accessed=7_000_000, transcendentals=0),
        name="turn",
    )(slots, *around, *across)

    vmem = pl.BlockSpec(memory_space=pltpu.VMEM)
    ampt, dens, right = pl.pallas_call(
        amp_kernel,
        in_specs=[SMEM, SMEM, vmem, vmem, vmem] + [ANY] * 8,
        out_specs=[vmem, vmem, ANY],
        out_shape=[
            jax.ShapeDtypeStruct((2, 2 * v, 2 * v), BF16),
            jax.ShapeDtypeStruct((v, v), F32),
            jax.ShapeDtypeStruct((2, 8 * rows, 2 * v), BF16),
        ],
        scratch_shapes=[
            pltpu.VMEM((2, 8 * rows, 2 * v), BF16),
            pltpu.VMEM((2 * v, 2 * v), F32),
            pltpu.VMEM((2 * v, 2 * v), BF16),
            pltpu.SemaphoreType.DMA((2,)),
            pltpu.SemaphoreType.DMA((2,)),
        ],
        cost_estimate=pl.CostEstimate(
            flops=6_200_000_000, bytes_accessed=20_000_000, transcendentals=0
        ),
        name="amplitudes",
    )(place, scal, left, vir_energy.reshape(1, -1), vir_energy.reshape(-1, 1), *sets_a, *sets_b)

    def gamma_part(s):
        at = 2 * ((y + s) % 4)
        slot = jnp.stack([at + c, at + 1 - c]).astype(jnp.int32)
        out = pl.pallas_call(
            gamma_kernel,
            grid_spec=pltpu.PrefetchScalarGridSpec(
                num_scalar_prefetch=1,
                grid=(2,),
                in_specs=[
                    SMEM,
                    pl.BlockSpec((2, rows, 2 * v), lambda n, slot: (0, slot[n], 0)),
                    pl.BlockSpec((2, 2 * v, 2 * v), lambda n, slot: (0, 0, 0)),
                ],
                out_specs=pl.BlockSpec((1, rows, 2 * v), lambda n, slot: (n, 0, 0)),
            ),
            out_shape=jax.ShapeDtypeStruct((2, rows, 2 * v), F32),
            cost_estimate=pl.CostEstimate(
                flops=1_360_000_000, bytes_accessed=6_000_000, transcendentals=0
            ),
            name="gamma",
        )(slot, scal, right, ampt)
        return out[0] + swap(out[1])

    sent = [move(gamma_part(s).astype(BF16), "y", s) for s in (2, 1, 3)]
    gamma = gamma_part(0)
    for part in sent:
        gamma = gamma + part.astype(F32)
    gamma_out = gamma.reshape(rows, orbitals, v)

    half = v // 2
    halves = dens.reshape(2, half, v)
    keep = lax.dynamic_index_in_dim(halves, c, 0, keepdims=False)
    give = lax.dynamic_index_in_dim(halves, 1 - c, 0, keepdims=False)
    part = (keep + swap(give)).reshape(4, half // 4, v)
    piece = lambda s: lax.dynamic_index_in_dim(part, (y + s) % 4, 0, keepdims=False)
    own = piece(0) + move(piece(1), "y", 1) + move(piece(3), "y", 3) + move(piece(2), "y", 2)
    own = four_sum(four_sum(own, "x"), "z") / task_iblock.shape[0]
    ring = jnp.stack([own] + [move(own, "y", s) for s in (1, 2, 3)])
    mine = ring[ys].reshape(half, v)
    other = swap(mine)
    density = jnp.where(c == 0, jnp.concatenate([mine, other]), jnp.concatenate([other, mine]))
    return gamma_out, density


def solution(mesh):
    finer = Mesh(mesh.devices.reshape(4, 4, 4, 2), AXES)
    placed = (P(OCOL, OROW, None), P(), P(), P(), P(), P())
    return jax.shard_map(
        local, mesh=finer, in_specs=placed, out_specs=(P(OCOL, OROW, None), P()), check_vma=False
    )
```

```python
import jax
import jax.numpy as jnp
from jax import lax
from jax.experimental import pallas as pl
from jax.experimental.pallas import tpu as pltpu
from jax.sharding import Mesh
from jax.sharding import PartitionSpec as P


AXES = ("z", "x", "y", "c")
OROW = ("z", "x")
OCOL = ("y", "c")
BF16 = jnp.bfloat16
F32 = jnp.float32
ANY = pl.BlockSpec(memory_space=pl.ANY)
SMEM = pl.BlockSpec(memory_space=pltpu.SMEM)


def move(x, axis, s):
    n = lax.axis_size(axis)
    return lax.ppermute(x, axis, [(i, (i + s) % n) for i in range(n)])


def swap(x):
    return lax.ppermute(x, "c", [(0, 1), (1, 0)])


def to_plane():
    pairs = []
    for z in range(4):
        for x in range(4):
            for y in range(4):
                for c in range(2):
                    source = ((z * 4 + x) * 4 + y) * 2 + c
                    target = (((2 * (z // 2) + c) * 4 + (x + y) % 4) * 4 + x) * 2 + z % 2
                    pairs.append((source, target))
    return pairs


def turn_kernel(slot_ref, *refs):
    pieces, out_ref, held, sem = refs[:8], refs[8], refs[9], refs[10]
    rows = pieces[0].shape[1]
    copies = [
        pltpu.make_async_copy(
            piece, held.at[:, pl.ds(pl.multiple_of(slot_ref[n] * rows, rows), rows), :], sem.at[n]
        )
        for n, piece in enumerate(pieces)
    ]
    for copy in copies:
        copy.start()
    for copy in copies:
        copy.wait()
    v = held.shape[2]
    for i in range(2):
        out_ref[i * v : (i + 1) * v, :] = held[i].T


def amp_kernel(place_ref, scal_ref, left_ref, row_ref, col_ref, *refs):
    sets_a, sets_b = refs[0:4], refs[4:8]
    ampt_ref, dens_ref, right_ref = refs[8:11]
    held, k_ref, amp_ref, sem, out_sem = refs[11:]
    rows, v = sets_a[0].shape[1:]

    def piece(source, slot, h, half):
        at = pl.ds(pl.multiple_of(slot * rows, rows), rows)
        return pltpu.make_async_copy(
            source, held.at[h, at, half * v : (half + 1) * v], sem.at[h]
        )

    for s in range(4):
        for t in range(4):
            for source, zs, xs, half in ((sets_a[s], s, t, 0), (sets_b[s], t, s, 1)):
                zz = place_ref[zs]
                piece(
                    source.at[t], 2 * place_ref[4 + xs] + lax.rem(zz, 2), zz // 2, half
                ).start()
    for h in range(2):
        for _ in range(16):
            piece(sets_a[0].at[0], 0, h, 0).wait()
        copy_out = pltpu.make_async_copy(held.at[h], right_ref.at[h], out_sem.at[h])
        copy_out.start()
        k_ref[...] = jnp.dot(left_ref[...], held[h], preferred_element_type=F32)
        for i in range(2):
            for j in range(2):
                a, b = slice(i * v, (i + 1) * v), slice(j * v, (j + 1) * v)
                k = k_ref[a, b]
                kt = k.T
                pair = scal_ref[i] + scal_ref[2 + 2 * h + j]
                both = scal_ref[10 + i] * scal_ref[12 + 2 * h + j]
                delta = (pair - col_ref[...]) - row_ref[...]
                amp_ref[a, b] = (both * ((2.0 * k - kt) / delta)).astype(BF16)
                ampt_ref[h, b, a] = (both * ((2.0 * kt - k) / delta)).astype(BF16)
        part = None
        for i in range(2):
            a = slice(i * v, (i + 1) * v)
            prod = jnp.dot(amp_ref[a, :], ampt_ref[h, :, a], preferred_element_type=F32)
            part = prod if part is None else part + prod
        part = scal_ref[6 + h] * part
        if h == 0:
            dens_ref[...] = part
        else:
            dens_ref[...] += part
    for h in range(2):
        pltpu.make_async_copy(held.at[h], right_ref.at[h], out_sem.at[h]).wait()


def gamma_kernel(slot_ref, scal_ref, mine_ref, other_ref, ampt_ref, keep_ref, give_ref):
    for right_ref, out_ref in ((other_ref, give_ref), (mine_ref, keep_ref)):
        total = scal_ref[8] * jnp.dot(right_ref[0], ampt_ref[0], preferred_element_type=F32)
        out_ref[0] = total + scal_ref[9] * jnp.dot(
            right_ref[1], ampt_ref[1], preferred_element_type=F32
        )


def swap_bits(x, axis, bits):
    return lax.ppermute(x, axis, [(i, i ^ bits) for i in range(lax.axis_size(axis))])


def halves_of(x, second):
    low, high = jnp.split(x, 2)
    return jnp.where(second, high, low), jnp.where(second, low, high)


def joined(mine, other, second):
    return jnp.where(
        second, jnp.concatenate([other, mine]), jnp.concatenate([mine, other])
    )


def local(integrals, occ_count, occ_energy, vir_energy, task_iblock, task_jblock):
    rows, orbitals, v = integrals.shape
    z, x, y, c = (lax.axis_index(a) for a in AXES)
    my_row = z * 4 + x
    steps = jnp.arange(4)
    shard = jnp.swapaxes(integrals, 0, 1)

    planed = lax.ppermute(shard, AXES, to_plane())
    shard, planed = lax.optimization_barrier((shard, planed))
    around = [shard] + [move(shard, "y", s) for s in (1, 2, 3)]
    across = [swap(p) for p in around]
    first_a = jnp.stack([planed[0]] + [move(planed[0], "x", s) for s in (1, 2, 3)])
    first_b = jnp.stack([planed[1]] + [move(planed[1], "z", s) for s in (1, 2, 3)])
    sets_a = [first_a] + [move(first_a, "z", s) for s in (1, 2, 3)]
    sets_b = [first_b] + [move(first_b, "x", s) for s in (1, 2, 3)]

    ys = (y - steps) % 4
    slots = jnp.concatenate([2 * ys + c, 2 * ys + 1 - c]).astype(jnp.int32)
    place = jnp.concatenate([(z - steps) % 4, (x - steps - y) % 4]).astype(jnp.int32)
    blocks = 4 * (2 * jnp.arange(2) + c) + y
    first, second = task_iblock[:, 0], task_jblock
    ours = ((first == my_row)[:, None] & (second[:, None] == blocks[None])).sum(0)
    theirs = ((second == my_row)[:, None] & (first[:, None] == blocks[None])).sum(0)
    energy = occ_energy.reshape(-1, orbitals)
    used = jnp.arange(orbitals)[None, :] < occ_count[:, None]
    scal = jnp.concatenate(
        [
            energy[my_row],
            energy[blocks].reshape(-1),
            ours.astype(F32),
            (ours + theirs).astype(F32),
            used[my_row].astype(F32),
            used[blocks].reshape(-1).astype(F32),
        ]
    )

    left = pl.pallas_call(
        turn_kernel,
        in_specs=[SMEM] + [ANY] * 8,
        out_specs=pl.BlockSpec(memory_space=pltpu.VMEM),
        out_shape=jax.ShapeDtypeStruct((2 * v, 8 * rows), BF16),
        scratch_shapes=[pltpu.VMEM((2, 8 * rows, v), BF16), pltpu.SemaphoreType.DMA((8,))],
        cost_estimate=pl.CostEstimate(flops=0, bytes_accessed=7_000_000, transcendentals=0),
        name="turn",
    )(slots, *around, *across)

    vmem = pl.BlockSpec(memory_space=pltpu.VMEM)
    ampt, dens, right = pl.pallas_call(
        amp_kernel,
        in_specs=[SMEM, SMEM, vmem, vmem, vmem] + [ANY] * 8,
        out_specs=[vmem, vmem, ANY],
        out_shape=[
            jax.ShapeDtypeStruct((2, 2 * v, 2 * v), BF16),
            jax.ShapeDtypeStruct((v, v), F32),
            jax.ShapeDtypeStruct((2, 8 * rows, 2 * v), BF16),
        ],
        scratch_shapes=[
            pltpu.VMEM((2, 8 * rows, 2 * v), BF16),
            pltpu.VMEM((2 * v, 2 * v), F32),
            pltpu.VMEM((2 * v, 2 * v), BF16),
            pltpu.SemaphoreType.DMA((2,)),
            pltpu.SemaphoreType.DMA((2,)),
        ],
        cost_estimate=pl.CostEstimate(
            flops=6_200_000_000, bytes_accessed=20_000_000, transcendentals=0
        ),
        name="amplitudes",
    )(place, scal, left, vir_energy.reshape(1, -1), vir_energy.reshape(-1, 1), *sets_a, *sets_b)

    def gamma_parts(ends):
        at = 2 * ((y + jnp.array(ends)) % 4)
        slot = jnp.stack([at + c, at + 1 - c]).astype(jnp.int32)
        width = 2 * v
        return pl.pallas_call(
            gamma_kernel,
            grid_spec=pltpu.PrefetchScalarGridSpec(
                num_scalar_prefetch=1,
                grid=(len(ends),),
                in_specs=[
                    SMEM,
                    pl.BlockSpec((2, rows, width), lambda n, slot: (0, slot[0, n], 0)),
                    pl.BlockSpec((2, rows, width), lambda n, slot: (0, slot[1, n], 0)),
                    pl.BlockSpec((2, width, width), lambda n, slot: (0, 0, 0)),
                ],
                out_specs=[pl.BlockSpec((1, rows, width), lambda n, slot: (n, 0, 0))] * 2,
            ),
            out_shape=[jax.ShapeDtypeStruct((len(ends), rows, width), F32)] * 2,
            cost_estimate=pl.CostEstimate(
                flops=1_360_000_000 * len(ends), bytes_accessed=10_000_000, transcendentals=0
            ),
        )(slot, scal, right, right, ampt)

    low, high = halves_of(dens, c == 1)
    dens_got = swap(high)
    keep, give = gamma_parts((2, 1))
    got = swap(give)
    keep_near, give_near = gamma_parts((3, 0))
    got_near = swap(give_near)
    to_far, to_next = (keep[0] + got[0]).astype(BF16), (keep[1] + got[1]).astype(BF16)
    far = move(to_far, "y", 2)
    next_one = move(to_next, "y", 1)
    to_last = (keep_near[0] + got_near[0]).astype(BF16)
    last_one = move(to_last, "y", 3)
    gamma = keep_near[1] + got_near[1]
    gamma = gamma + next_one.astype(F32) + last_one.astype(F32) + far.astype(F32)
    gamma_out = gamma.reshape(rows, orbitals, v)

    own = low + dens_got
    upper, odd = y // 2 == 1, y % 2 == 1
    for bits, second in ((3, upper), (1, odd)):
        own, sent = halves_of(own, second)
        got = swap_bits(sent, "y", bits)
        own = own + got
    for axis in ("x", "z"):
        for bits in (1, 3):
            got = swap_bits(own, axis, bits)
            own = own + got
    own = own / task_iblock.shape[0]
    for bits, second in ((1, odd), (3, upper)):
        got = swap_bits(own, "y", bits)
        own = joined(own, got, second)
    got = swap(own)
    density = joined(own, got, c == 1)
    return gamma_out, density


def solution(mesh):
    finer = Mesh(mesh.devices.reshape(4, 4, 4, 2), AXES)
    placed = (P(OCOL, OROW, None), P(), P(), P(), P(), P())
    return jax.shard_map(
        local, mesh=finer, in_specs=placed, out_specs=(P(OCOL, OROW, None), P()), check_vma=False
    )
```

```python
import jax
import jax.numpy as jnp
from jax import lax
from jax.experimental import pallas as pl
from jax.experimental.pallas import tpu as pltpu
from jax.sharding import Mesh
from jax.sharding import PartitionSpec as P


AXES = ("z", "x", "y", "c")
OROW = ("z", "x")
OCOL = ("y", "c")
BF16 = jnp.bfloat16
F32 = jnp.float32
ANY = pl.BlockSpec(memory_space=pl.ANY)
SMEM = pl.BlockSpec(memory_space=pltpu.SMEM)


def move(x, axis, s):
    n = lax.axis_size(axis)
    return lax.ppermute(x, axis, [(i, (i + s) % n) for i in range(n)])


def swap(x):
    return lax.ppermute(x, "c", [(0, 1), (1, 0)])


def to_plane():
    pairs = []
    for z in range(4):
        for x in range(4):
            for y in range(4):
                for c in range(2):
                    source = ((z * 4 + x) * 4 + y) * 2 + c
                    target = (((2 * (z // 2) + c) * 4 + (x + y) % 4) * 4 + x) * 2 + z % 2
                    pairs.append((source, target))
    return pairs


def turn_kernel(slot_ref, *refs):
    pieces, out_ref, held, sem = refs[:8], refs[8], refs[9], refs[10]
    rows = pieces[0].shape[1]
    copies = [
        pltpu.make_async_copy(
            piece, held.at[:, pl.ds(pl.multiple_of(slot_ref[n] * rows, rows), rows), :], sem.at[n]
        )
        for n, piece in enumerate(pieces)
    ]
    for copy in copies:
        copy.start()
    for copy in copies:
        copy.wait()
    v = held.shape[2]
    for i in range(2):
        out_ref[i * v : (i + 1) * v, :] = held[i].T


def amp_kernel(place_ref, scal_ref, left_ref, row_ref, col_ref, *refs):
    sets_a, sets_b = refs[0:4], refs[4:8]
    right_ref, ampt_ref, keep_ref, give_ref = refs[8:12]
    held, k_ref, amp_ref, dens_ref, sem, out_sem = refs[12:]
    rows, v = sets_a[0].shape[1:]

    def piece(source, slot, h, half):
        at = pl.ds(pl.multiple_of(slot * rows, rows), rows)
        return pltpu.make_async_copy(
            source, held.at[h, at, half * v : (half + 1) * v], sem.at[h]
        )

    for s in range(4):
        for t in range(4):
            for source, zs, xs, half in ((sets_a[s], s, t, 0), (sets_b[s], t, s, 1)):
                zz = place_ref[zs]
                piece(
                    source.at[t], 2 * place_ref[4 + xs] + lax.rem(zz, 2), zz // 2, half
                ).start()
    for h in range(2):
        for _ in range(16):
            piece(sets_a[0].at[0], 0, h, 0).wait()
        pltpu.make_async_copy(held.at[h], right_ref.at[h], out_sem.at[h]).start()
        k_ref[...] = jnp.dot(left_ref[...], held[h], preferred_element_type=F32)
        for i in range(2):
            for j in range(2):
                a, b = slice(i * v, (i + 1) * v), slice(j * v, (j + 1) * v)
                k = k_ref[a, b]
                kt = k.T
                pair = scal_ref[i] + scal_ref[2 + 2 * h + j]
                both = scal_ref[10 + i] * scal_ref[12 + 2 * h + j]
                delta = (pair - col_ref[...]) - row_ref[...]
                amp_ref[a, b] = (both * ((2.0 * k - kt) / delta)).astype(BF16)
                ampt_ref[h, b, a] = (both * ((2.0 * kt - k) / delta)).astype(BF16)
        part = None
        for i in range(2):
            a = slice(i * v, (i + 1) * v)
            prod = jnp.dot(amp_ref[a, :], ampt_ref[h, :, a], preferred_element_type=F32)
            part = prod if part is None else part + prod
        part = scal_ref[6 + h] * part
        if h == 0:
            dens_ref[...] = part
        else:
            dens_ref[...] += part
    chunk = v // 8
    for n in range(8):
        start = pl.multiple_of(place_ref[8 + n] * chunk, 8)
        out_ref = keep_ref if n < 4 else give_ref
        out_ref[(n % 4) * chunk : (n % 4 + 1) * chunk, :] = dens_ref[pl.ds(start, chunk), :]
    for h in range(2):
        pltpu.make_async_copy(held.at[h], right_ref.at[h], out_sem.at[h]).wait()


def gamma_kernel(slot_ref, scal_ref, right_ref, ampt_ref, keep_ref, give_ref, both_ref):
    rows = keep_ref.shape[1]
    both_ref[...] = scal_ref[8] * jnp.dot(
        right_ref[0], ampt_ref[0], preferred_element_type=F32
    ) + scal_ref[9] * jnp.dot(right_ref[1], ampt_ref[1], preferred_element_type=F32)
    for out_ref, side in ((keep_ref, slot_ref[2]), (give_ref, 1 - slot_ref[2])):
        out_ref[0] = both_ref[pl.ds(pl.multiple_of(side * rows, rows), rows), :]


def place_kernel(place_ref, mine_ref, other_ref, out_ref):
    chunk = out_ref.shape[0] // 8
    for n in range(8):
        ref = mine_ref if n < 4 else other_ref
        start = pl.multiple_of(place_ref[8 + n] * chunk, 8)
        out_ref[pl.ds(start, chunk), :] = ref[(n % 4) * chunk : (n % 4 + 1) * chunk, :]


def swap_bits(x, axis, bits):
    return lax.ppermute(x, axis, [(i, i ^ bits) for i in range(lax.axis_size(axis))])


def local(integrals, occ_count, occ_energy, vir_energy, task_iblock, task_jblock):
    rows, orbitals, v = integrals.shape
    z, x, y, c = (lax.axis_index(a) for a in AXES)
    my_row = z * 4 + x
    steps = jnp.arange(4)
    shard = jnp.swapaxes(integrals, 0, 1)

    planed = lax.ppermute(shard, AXES, to_plane())
    shard, planed = lax.optimization_barrier((shard, planed))
    around = [shard]
    for s in (1, 2, 3):
        around.append(move(shard, "y", s))
    across = [swap(p) for p in around]
    first_a = jnp.stack([planed[0]] + [move(planed[0], "x", s) for s in (1, 2, 3)])
    first_b = jnp.stack([planed[1]] + [move(planed[1], "z", s) for s in (1, 2, 3)])
    sets_a = [first_a] + [move(first_a, "z", s) for s in (1, 2, 3)]
    sets_b = [first_b]
    for s in (1, 2, 3):
        sets_b.append(move(first_b, "x", s))

    ys = (y - steps) % 4
    slots = jnp.concatenate([2 * ys + c, 2 * ys + 1 - c]).astype(jnp.int32)
    chunks = y ^ jnp.array([0, 1, 3, 2])
    place = jnp.concatenate(
        [(z - steps) % 4, (x - steps - y) % 4, 4 * c + chunks, 4 - 4 * c + chunks]
    ).astype(jnp.int32)
    blocks = 4 * (2 * jnp.arange(2) + c) + y
    first, second = task_iblock[:, 0], task_jblock
    ours = ((first == my_row)[:, None] & (second[:, None] == blocks[None])).sum(0)
    theirs = ((second == my_row)[:, None] & (first[:, None] == blocks[None])).sum(0)
    energy = occ_energy.reshape(-1, orbitals)
    used = jnp.arange(orbitals)[None, :] < occ_count[:, None]
    scal = jnp.concatenate(
        [
            energy[my_row],
            energy[blocks].reshape(-1),
            ours.astype(F32),
            (ours + theirs).astype(F32),
            used[my_row].astype(F32),
            used[blocks].reshape(-1).astype(F32),
        ]
    )

    vmem = pl.BlockSpec(memory_space=pltpu.VMEM)
    left = pl.pallas_call(
        turn_kernel,
        in_specs=[SMEM] + [ANY] * 8,
        out_specs=vmem,
        out_shape=pltpu.VMEM((2 * v, 8 * rows), BF16),
        scratch_shapes=[pltpu.VMEM((2, 8 * rows, v), BF16), pltpu.SemaphoreType.DMA((8,))],
        compiler_params=pltpu.CompilerParams(vmem_limit_bytes=24 * 2**20),
        cost_estimate=pl.CostEstimate(flops=0, bytes_accessed=7_000_000, transcendentals=0),
        name="turn",
    )(slots, *around, *across)

    right, ampt, dens_keep, dens_give = pl.pallas_call(
        amp_kernel,
        in_specs=[SMEM, SMEM, vmem, vmem, vmem] + [ANY] * 8,
        out_specs=[ANY] + [vmem] * 3,
        out_shape=[
            jax.ShapeDtypeStruct((2, 8 * rows, 2 * v), BF16),
            jax.ShapeDtypeStruct((2, 2 * v, 2 * v), BF16),
            jax.ShapeDtypeStruct((v // 2, v), F32),
            jax.ShapeDtypeStruct((v // 2, v), F32),
        ],
        scratch_shapes=[
            pltpu.VMEM((2, 8 * rows, 2 * v), BF16),
            pltpu.VMEM((2 * v, 2 * v), F32),
            pltpu.VMEM((2 * v, 2 * v), BF16),
            pltpu.VMEM((v, v), F32),
            pltpu.SemaphoreType.DMA((2,)),
            pltpu.SemaphoreType.DMA((2,)),
        ],
        compiler_params=pltpu.CompilerParams(vmem_limit_bytes=62_900_000),
        cost_estimate=pl.CostEstimate(
            flops=6_200_000_000, bytes_accessed=12_000_000, transcendentals=0
        ),
        name="amplitudes",
    )(place, scal, left, vir_energy.reshape(1, -1), vir_energy.reshape(-1, 1), *sets_a, *sets_b)

    def gamma_parts(ends):
        slot = jnp.stack([(y + s) % 4 for s in ends] + [c]).astype(jnp.int32)
        width = 2 * v
        return pl.pallas_call(
            gamma_kernel,
            grid_spec=pltpu.PrefetchScalarGridSpec(
                num_scalar_prefetch=1,
                grid=(2,),
                in_specs=[
                    SMEM,
                    pl.BlockSpec((2, 2 * rows, width), lambda n, slot: (0, slot[n], 0)),
                    pl.BlockSpec((2, width, width), lambda n, slot: (0, 0, 0)),
                ],
                out_specs=[pl.BlockSpec((1, rows, width), lambda n, slot: (n, 0, 0))] * 2,
                scratch_shapes=[pltpu.VMEM((2 * rows, width), F32)],
            ),
            out_shape=[jax.ShapeDtypeStruct((2, rows, width), F32)] * 2,
            compiler_params=pltpu.CompilerParams(vmem_limit_bytes=62_000_000),
            cost_estimate=pl.CostEstimate(
                flops=2_720_000_000, bytes_accessed=4_000_000, transcendentals=0
            ),
        )(slot, scal, right, ampt)

    got = swap(dens_give)
    own = dens_keep + got
    keep, give = gamma_parts((2, 1))
    got_far = swap(give)
    keep_near, give_near = gamma_parts((3, 0))
    got_near = swap(give_near)
    to_far, to_next = (keep[0] + got_far[0]).astype(BF16), (keep[1] + got_far[1]).astype(BF16)
    far = move(to_far, "y", 2)
    next_one = move(to_next, "y", 1)
    to_last = (keep_near[0] + got_near[0]).astype(BF16)
    last_one = move(to_last, "y", 3)
    gamma = keep_near[1] + got_near[1]
    gamma = gamma + next_one.astype(F32) + last_one.astype(F32) + far.astype(F32)
    gamma_out = gamma.reshape(rows, orbitals, v)

    for bits in (3, 1):
        mine, sent = jnp.split(own, 2)
        got = swap_bits(sent, "y", bits)
        own = mine + got
    for axis in ("x", "z"):
        for bits in (1, 3):
            got = swap_bits(own, axis, bits)
            own = own + got
    own = own / task_iblock.shape[0]
    for bits in (1, 3):
        got = swap_bits(own, "y", bits)
        own = jnp.concatenate([own, got])
    got = swap(own)
    density = pl.pallas_call(
        place_kernel,
        in_specs=[SMEM, vmem, vmem],
        out_specs=vmem,
        out_shape=jax.ShapeDtypeStruct((v, v), F32),
        compiler_params=pltpu.CompilerParams(vmem_limit_bytes=4 * 2**20),
        name="place",
    )(place, own, got)
    return gamma_out, density


def solution(mesh):
    finer = Mesh(mesh.devices.reshape(4, 4, 4, 2), AXES)
    placed = (P(OCOL, OROW, None), P(), P(), P(), P(), P())
    return jax.shard_map(
        local, mesh=finer, in_specs=placed, out_specs=(P(OCOL, OROW, None), P()), check_vma=False
    )
```

```python
import jax
import jax.numpy as jnp
from jax import lax
from jax.experimental import pallas as pl
from jax.experimental.pallas import tpu as pltpu
from jax.sharding import Mesh
from jax.sharding import PartitionSpec as P


AXES = ("z", "x", "y", "c")
OROW = ("z", "x")
OCOL = ("y", "c")
BF16 = jnp.bfloat16
F32 = jnp.float32
ANY = pl.BlockSpec(memory_space=pl.ANY)
SMEM = pl.BlockSpec(memory_space=pltpu.SMEM)


def move(x, axis, s):
    n = lax.axis_size(axis)
    return lax.ppermute(x, axis, [(i, (i + s) % n) for i in range(n)])


def swap(x):
    return lax.ppermute(x, "c", [(0, 1), (1, 0)])


def to_plane(turn):
    pairs = []
    for z in range(4):
        for x in range(4):
            for y in range(4):
                for c in range(2):
                    source = ((z * 4 + x) * 4 + y) * 2 + c
                    target = (((2 * (z // 2) + c) * 4 + (x + turn * y) % 4) * 4 + x) * 2 + z % 2
                    pairs.append((source, target))
    return pairs


def turn_kernel(slot_ref, *refs):
    pieces, out_ref, held, sem = refs[:8], refs[8], refs[9], refs[10]
    rows = pieces[0].shape[1]
    copies = [
        pltpu.make_async_copy(
            piece, held.at[:, pl.ds(pl.multiple_of(slot_ref[n] * rows, rows), rows), :], sem.at[n]
        )
        for n, piece in enumerate(pieces)
    ]
    for copy in copies:
        copy.start()
    for copy in copies:
        copy.wait()
    v = held.shape[2]
    for i in range(2):
        out_ref[i * v : (i + 1) * v, :] = held[i].T


def pair_kernel(place_ref, scal_ref, left_ref, row_ref, col_ref, *refs):
    sets_a, sets_b = refs[0:4], refs[4:8]
    parts = (refs[8:10], refs[10:12])
    dens_keep, dens_give = refs[12:14]
    held, own_ref, k_ref, amp_ref, ampt_ref, dens_ref, both_ref, sem, out_sem = refs[14:]
    rows, v = sets_a[0].shape[1:]

    def piece(source, slot, h, half):
        at = pl.ds(pl.multiple_of(slot * rows, rows), rows)
        return pltpu.make_async_copy(
            source, held.at[h, at, half * v : (half + 1) * v], sem.at[h]
        )

    fetch = pltpu.make_async_copy(left_ref, own_ref, sem.at[2])
    fetch.start()
    for s in range(4):
        for t in range(4):
            for source, zs, ys, half in (
                (sets_a[s], s, 4 + t, 0),
                (sets_b[s], t, 8 + s, 1),
            ):
                zz = place_ref[zs]
                piece(source.at[t], 2 * place_ref[ys] + lax.rem(zz, 2), zz // 2, half).start()
    fetch.wait()
    for h in range(2):
        for _ in range(16):
            piece(sets_a[0].at[0], 0, h, 0).wait()
        k_ref[...] = jnp.dot(own_ref[...], held[h], preferred_element_type=F32)
        for i in range(2):
            for j in range(2):
                a, b = slice(i * v, (i + 1) * v), slice(j * v, (j + 1) * v)
                k = k_ref[a, b]
                kt = k.T
                pair = scal_ref[i] + scal_ref[2 + 2 * h + j]
                both = scal_ref[10 + i] * scal_ref[12 + 2 * h + j]
                delta = (pair - col_ref[...]) - row_ref[...]
                amp_ref[a, b] = (both * ((2.0 * k - kt) / delta)).astype(BF16)
                ampt_ref[h, b, a] = (both * ((2.0 * kt - k) / delta)).astype(BF16)
        part = None
        for i in range(2):
            a = slice(i * v, (i + 1) * v)
            prod = jnp.dot(amp_ref[a, :], ampt_ref[h, :, a], preferred_element_type=F32)
            part = prod if part is None else part + prod
        part = scal_ref[6 + h] * part
        if h == 0:
            dens_ref[...] = part
        else:
            dens_ref[...] += part

    def leave(n, side):
        core = place_ref[24] if side == 0 else 1 - place_ref[24]
        return pltpu.make_async_copy(
            both_ref.at[n % 2, pl.ds(pl.multiple_of(core * rows, rows), rows), :],
            parts[n // 2][side].at[n % 2],
            out_sem.at[n % 2, side],
        )

    for n in range(4):
        if n >= 2:
            leave(n - 2, 0).wait()
            leave(n - 2, 1).wait()
        at = pl.ds(pl.multiple_of(place_ref[20 + n] * rows, rows), 2 * rows)
        both_ref[n % 2] = scal_ref[8] * jnp.dot(
            held[0, at, :], ampt_ref[0], preferred_element_type=F32
        ) + scal_ref[9] * jnp.dot(held[1, at, :], ampt_ref[1], preferred_element_type=F32)
        leave(n, 1).start()
        leave(n, 0).start()
    chunk = v // 8
    for n in range(8):
        start = pl.multiple_of(place_ref[12 + n] * chunk, 8)
        out_ref = dens_keep if n < 4 else dens_give
        out_ref[(n % 4) * chunk : (n % 4 + 1) * chunk, :] = dens_ref[pl.ds(start, chunk), :]
    for n in (2, 3):
        leave(n, 1).wait()
        leave(n, 0).wait()


def place_kernel(place_ref, mine_ref, other_ref, out_ref):
    chunk = out_ref.shape[0] // 8
    for n in range(8):
        ref = mine_ref if n < 4 else other_ref
        start = pl.multiple_of(place_ref[12 + n] * chunk, 8)
        out_ref[pl.ds(start, chunk), :] = ref[(n % 4) * chunk : (n % 4 + 1) * chunk, :]


def swap_bits(x, axis, bits):
    return lax.ppermute(x, axis, [(i, i ^ bits) for i in range(lax.axis_size(axis))])


def local(integrals, occ_count, occ_energy, vir_energy, task_iblock, task_jblock):
    rows, orbitals, v = integrals.shape
    z, x, y, c = (lax.axis_index(a) for a in AXES)
    my_row = z * 4 + x
    steps = jnp.arange(4)
    shard = jnp.swapaxes(integrals, 0, 1)

    plane_a = lax.ppermute(shard[0], AXES, to_plane(1))
    plane_b = lax.ppermute(shard[1], AXES, to_plane(-1))
    around = [shard]
    for s in (1, 2, 3):
        around.append(move(shard, "y", s))
    across = [swap(p) for p in around]
    sets = []
    for half, near, far in ((plane_a, "x", "z"), (plane_b, "z", "x")):
        first = [half]
        for s in (1, 2, 3):
            first.append(move(half, near, s))
        first = jnp.stack(first)
        sets.append([first])
        for s in (1, 2, 3):
            sets[-1].append(move(first, far, s))
    sets_a, sets_b = sets

    ys = (y - steps) % 4
    slots = jnp.concatenate([2 * ys + c, 2 * ys + 1 - c]).astype(jnp.int32)
    chunks = y ^ jnp.array([0, 1, 3, 2])
    place = jnp.concatenate(
        [
            (z - steps) % 4,
            (x - steps - y) % 4,
            (y - x + steps) % 4,
            4 * c + chunks,
            4 - 4 * c + chunks,
            2 * ((y + jnp.array([2, 1, 3, 0])) % 4),
            c[None],
        ]
    ).astype(jnp.int32)
    blocks = 4 * (2 * jnp.arange(2) + c) + y
    first, second = task_iblock[:, 0], task_jblock
    ours = ((first == my_row)[:, None] & (second[:, None] == blocks[None])).sum(0)
    theirs = ((second == my_row)[:, None] & (first[:, None] == blocks[None])).sum(0)
    energy = occ_energy.reshape(-1, orbitals)
    used = jnp.arange(orbitals)[None, :] < occ_count[:, None]
    scal = jnp.concatenate(
        [
            energy[my_row],
            energy[blocks].reshape(-1),
            ours.astype(F32),
            (ours + theirs).astype(F32),
            used[my_row].astype(F32),
            used[blocks].reshape(-1).astype(F32),
        ]
    )

    vmem = pl.BlockSpec(memory_space=pltpu.VMEM)
    left = pl.pallas_call(
        turn_kernel,
        in_specs=[SMEM] + [ANY] * 8,
        out_specs=vmem,
        out_shape=jax.ShapeDtypeStruct((2 * v, 8 * rows), BF16),
        scratch_shapes=[pltpu.VMEM((2, 8 * rows, v), BF16), pltpu.SemaphoreType.DMA((8,))],
        compiler_params=pltpu.CompilerParams(vmem_limit_bytes=24 * 2**20),
        cost_estimate=pl.CostEstimate(flops=0, bytes_accessed=7_000_000, transcendentals=0),
        name="turn",
    )(slots, *around, *across)

    part = jax.ShapeDtypeStruct((2, rows, 2 * v), F32)
    half = jax.ShapeDtypeStruct((v // 2, v), F32)
    keep, give, keep_near, give_near, dens_keep, dens_give = pl.pallas_call(
        pair_kernel,
        in_specs=[SMEM, SMEM, ANY, vmem, vmem] + [ANY] * 8,
        out_specs=[ANY] * 4 + [vmem] * 2,
        out_shape=[part] * 4 + [half] * 2,
        scratch_shapes=[
            pltpu.VMEM((2, 8 * rows, 2 * v), BF16),
            pltpu.VMEM((2 * v, 8 * rows), BF16),
            pltpu.VMEM((2 * v, 2 * v), F32),
            pltpu.VMEM((2 * v, 2 * v), BF16),
            pltpu.VMEM((2, 2 * v, 2 * v), BF16),
            pltpu.VMEM((v, v), F32),
            pltpu.VMEM((2, 2 * rows, 2 * v), F32),
            pltpu.SemaphoreType.DMA((3,)),
            pltpu.SemaphoreType.DMA((2, 2)),
        ],
        compiler_params=pltpu.CompilerParams(vmem_limit_bytes=62_000_000),
        cost_estimate=pl.CostEstimate(
            flops=11_800_000_000, bytes_accessed=18_000_000, transcendentals=0
        ),
        name="pairs",
    )(place, scal, left, vir_energy.reshape(1, -1), vir_energy.reshape(-1, 1), *sets_a, *sets_b)

    got = swap(dens_give)
    own = dens_keep + got
    got_far = swap(give)
    got_near = swap(give_near)
    to_far, to_next = (keep[0] + got_far[0]).astype(BF16), (keep[1] + got_far[1]).astype(BF16)
    far = move(to_far, "y", 2)
    next_one = move(to_next, "y", 1)
    to_last = (keep_near[0] + got_near[0]).astype(BF16)
    last_one = move(to_last, "y", 3)
    gamma = keep_near[1] + got_near[1]
    gamma = gamma + next_one.astype(F32) + last_one.astype(F32) + far.astype(F32)
    gamma_out = gamma.reshape(rows, orbitals, v)

    for bits in (3, 1):
        mine, sent = jnp.split(own, 2)
        got = swap_bits(sent, "y", bits)
        own = mine + got
    for axis in ("x", "z"):
        for bits in (1, 3):
            got = swap_bits(own, axis, bits)
            own = own + got
    own = own / task_iblock.shape[0]
    for bits in (1, 3):
        got = swap_bits(own, "y", bits)
        own = jnp.concatenate([own, got])
    got = swap(own)
    density = pl.pallas_call(
        place_kernel,
        in_specs=[SMEM, vmem, vmem],
        out_specs=vmem,
        out_shape=jax.ShapeDtypeStruct((v, v), F32),
        compiler_params=pltpu.CompilerParams(vmem_limit_bytes=4 * 2**20),
        name="place",
    )(place, own, got)
    return gamma_out, density


def solution(mesh):
    finer = Mesh(mesh.devices.reshape(4, 4, 4, 2), AXES)
    placed = (P(OCOL, OROW, None), P(), P(), P(), P(), P())
    return jax.shard_map(
        local, mesh=finer, in_specs=placed, out_specs=(P(OCOL, OROW, None), P()), check_vma=False
    )
```

```python
import jax
import jax.numpy as jnp
from jax import lax
from jax.experimental import pallas as pl
from jax.experimental.pallas import tpu as pltpu
from jax.sharding import Mesh
from jax.sharding import PartitionSpec as P


AXES = ("z", "x", "y", "c")
OROW = ("z", "x")
OCOL = ("y", "c")
BF16 = jnp.bfloat16
F32 = jnp.float32
ANY = pl.BlockSpec(memory_space=pl.ANY)
SMEM = pl.BlockSpec(memory_space=pltpu.SMEM)


def move(x, axis, s):
    n = lax.axis_size(axis)
    return lax.ppermute(x, axis, [(i, (i + s) % n) for i in range(n)])


def swap(x):
    return lax.ppermute(x, "c", [(0, 1), (1, 0)])


def to_plane(turn):
    pairs = []
    for z in range(4):
        for x in range(4):
            for y in range(4):
                for c in range(2):
                    source = ((z * 4 + x) * 4 + y) * 2 + c
                    target = (((2 * (z // 2) + c) * 4 + (x + turn * y) % 4) * 4 + x) * 2 + z % 2
                    pairs.append((source, target))
    return pairs


def turn_kernel(slot_ref, *refs):
    pieces, out_ref, held, sem = refs[:8], refs[8], refs[9], refs[10]
    rows = pieces[0].shape[1]
    copies = [
        pltpu.make_async_copy(
            piece, held.at[:, pl.ds(pl.multiple_of(slot_ref[n] * rows, rows), rows), :], sem.at[n]
        )
        for n, piece in enumerate(pieces)
    ]
    for copy in copies:
        copy.start()
    for copy in copies:
        copy.wait()
    v = held.shape[2]
    for i in range(2):
        out_ref[i * v : (i + 1) * v, :] = held[i].T


def pair_kernel(place_ref, scal_ref, left_ref, row_ref, col_ref, *refs):
    sets_a, sets_b = refs[0:4], refs[4:8]
    parts = (refs[8:10], refs[10:12])
    dens_keep, dens_give = refs[12:14]
    held, own_ref, k_ref, amp_ref, ampt_ref, dens_ref, both_ref, sem, out_sem = refs[14:]
    rows, v = sets_a[0].shape[1:]

    def piece(source, slot, h, half):
        at = pl.ds(pl.multiple_of(slot * rows, rows), rows)
        return pltpu.make_async_copy(
            source, held.at[h, at, half * v : (half + 1) * v], sem.at[h]
        )

    fetch = pltpu.make_async_copy(left_ref, own_ref, sem.at[2])
    fetch.start()
    for s in range(4):
        for t in range(4):
            for source, zs, ys, half in (
                (sets_a[s], s, 4 + t, 0),
                (sets_b[s], t, 8 + s, 1),
            ):
                zz = place_ref[zs]
                piece(source.at[t], 2 * place_ref[ys] + lax.rem(zz, 2), zz // 2, half).start()
    fetch.wait()
    for h in range(2):
        for _ in range(16):
            piece(sets_a[0].at[0], 0, h, 0).wait()
        k_ref[...] = jnp.dot(own_ref[...], held[h], preferred_element_type=F32)
        for i in range(2):
            for j in range(2):
                a, b = slice(i * v, (i + 1) * v), slice(j * v, (j + 1) * v)
                k = k_ref[a, b]
                kt = k.T
                pair = scal_ref[i] + scal_ref[2 + 2 * h + j]
                both = scal_ref[10 + i] * scal_ref[12 + 2 * h + j]
                delta = (pair - col_ref[...]) - row_ref[...]
                amp_ref[a, b] = (both * ((2.0 * k - kt) / delta)).astype(BF16)
                ampt_ref[h, b, a] = (both * ((2.0 * kt - k) / delta)).astype(BF16)
        part = None
        for i in range(2):
            a = slice(i * v, (i + 1) * v)
            prod = jnp.dot(amp_ref[a, :], ampt_ref[h, :, a], preferred_element_type=F32)
            part = prod if part is None else part + prod
        part = scal_ref[6 + h] * part
        if h == 0:
            dens_ref[...] = part
        else:
            dens_ref[...] += part

    def leave(n, side):
        core = place_ref[24] if side == 0 else 1 - place_ref[24]
        return pltpu.make_async_copy(
            both_ref.at[n % 2, pl.ds(pl.multiple_of(core * rows, rows), rows), :],
            parts[n // 2][side].at[n % 2],
            out_sem.at[n % 2, side],
        )

    for n in range(4):
        if n >= 2:
            leave(n - 2, 0).wait()
            leave(n - 2, 1).wait()
        at = pl.ds(pl.multiple_of(place_ref[20 + n] * rows, rows), 2 * rows)
        both_ref[n % 2] = scal_ref[8] * jnp.dot(
            held[0, at, :], ampt_ref[0], preferred_element_type=F32
        ) + scal_ref[9] * jnp.dot(held[1, at, :], ampt_ref[1], preferred_element_type=F32)
        leave(n, 1).start()
        leave(n, 0).start()
    chunk = v // 8
    for n in range(8):
        start = pl.multiple_of(place_ref[12 + n] * chunk, 8)
        out_ref = dens_keep if n < 4 else dens_give
        out_ref[(n % 4) * chunk : (n % 4 + 1) * chunk, :] = dens_ref[pl.ds(start, chunk), :]
    for n in (2, 3):
        leave(n, 1).wait()
        leave(n, 0).wait()


def place_kernel(place_ref, mine_ref, other_ref, out_ref):
    chunk = out_ref.shape[0] // 8
    for n in range(8):
        ref = mine_ref if n < 4 else other_ref
        start = pl.multiple_of(place_ref[12 + n] * chunk, 8)
        out_ref[pl.ds(start, chunk), :] = ref[(n % 4) * chunk : (n % 4 + 1) * chunk, :]


def swap_bits(x, axis, bits):
    return lax.ppermute(x, axis, [(i, i ^ bits) for i in range(lax.axis_size(axis))])


def local(integrals, occ_count, occ_energy, vir_energy, task_iblock, task_jblock):
    rows, orbitals, v = integrals.shape
    z, x, y, c = (lax.axis_index(a) for a in AXES)
    my_row = z * 4 + x
    steps = jnp.arange(4)
    shard = jnp.swapaxes(integrals, 0, 1)

    plane_a = lax.ppermute(shard[0], AXES, to_plane(1))
    plane_b = lax.ppermute(shard[1], AXES, to_plane(-1))
    around = [shard]
    for s in (1, 2, 3):
        around.append(move(shard, "y", s))
    across = []
    for part in around:
        across.append(swap(part))
    sets = []
    for half, near, far in ((plane_a, "x", "z"), (plane_b, "z", "x")):
        first = [half]
        for s in (1, 2, 3):
            first.append(move(half, near, s))
        first = jnp.stack(first)
        sets.append([first])
        for s in (1, 2, 3):
            sets[-1].append(move(first, far, s))
    sets_a, sets_b = sets

    ys = (y - steps) % 4
    slots = jnp.concatenate([2 * ys + c, 2 * ys + 1 - c]).astype(jnp.int32)
    chunks = y ^ jnp.array([0, 1, 3, 2])
    place = jnp.concatenate(
        [
            (z - steps) % 4,
            (x - steps - y) % 4,
            (y - x + steps) % 4,
            4 * c + chunks,
            4 - 4 * c + chunks,
            2 * ((y + jnp.array([2, 1, 3, 0])) % 4),
            c[None],
        ]
    ).astype(jnp.int32)
    blocks = 4 * (2 * jnp.arange(2) + c) + y
    first, second = task_iblock[:, 0], task_jblock
    ours = ((first == my_row)[:, None] & (second[:, None] == blocks[None])).sum(0)
    theirs = ((second == my_row)[:, None] & (first[:, None] == blocks[None])).sum(0)
    energy = occ_energy.reshape(-1, orbitals)
    used = jnp.arange(orbitals)[None, :] < occ_count[:, None]
    scal = jnp.concatenate(
        [
            energy[my_row],
            energy[blocks].reshape(-1),
            ours.astype(F32),
            (ours + theirs).astype(F32),
            used[my_row].astype(F32),
            used[blocks].reshape(-1).astype(F32),
        ]
    )

    vmem = pl.BlockSpec(memory_space=pltpu.VMEM)
    left = pl.pallas_call(
        turn_kernel,
        in_specs=[SMEM] + [ANY] * 8,
        out_specs=vmem,
        out_shape=jax.ShapeDtypeStruct((2 * v, 8 * rows), BF16),
        scratch_shapes=[pltpu.VMEM((2, 8 * rows, v), BF16), pltpu.SemaphoreType.DMA((8,))],
        compiler_params=pltpu.CompilerParams(vmem_limit_bytes=24 * 2**20),
        cost_estimate=pl.CostEstimate(flops=0, bytes_accessed=7_000_000, transcendentals=0),
        name="turn",
    )(slots, *around, *across)

    part = jax.ShapeDtypeStruct((2, rows, 2 * v), F32)
    half = jax.ShapeDtypeStruct((v // 2, v), F32)
    keep, give, keep_near, give_near, dens_keep, dens_give = pl.pallas_call(
        pair_kernel,
        in_specs=[SMEM, SMEM, ANY, vmem, vmem] + [ANY] * 8,
        out_specs=[ANY] * 4 + [vmem] * 2,
        out_shape=[part] * 4 + [half] * 2,
        scratch_shapes=[
            pltpu.VMEM((2, 8 * rows, 2 * v), BF16),
            pltpu.VMEM((2 * v, 8 * rows), BF16),
            pltpu.VMEM((2 * v, 2 * v), F32),
            pltpu.VMEM((2 * v, 2 * v), BF16),
            pltpu.VMEM((2, 2 * v, 2 * v), BF16),
            pltpu.VMEM((v, v), F32),
            pltpu.VMEM((2, 2 * rows, 2 * v), F32),
            pltpu.SemaphoreType.DMA((3,)),
            pltpu.SemaphoreType.DMA((2, 2)),
        ],
        compiler_params=pltpu.CompilerParams(vmem_limit_bytes=36 * 2**20),
        cost_estimate=pl.CostEstimate(
            flops=11_800_000_000, bytes_accessed=18_000_000, transcendentals=0
        ),
        name="pairs",
    )(place, scal, left, vir_energy.reshape(1, -1), vir_energy.reshape(-1, 1), *sets_a, *sets_b)

    got = swap(dens_give)
    own = dens_keep + got
    got_far = swap(give)
    got_near = swap(give_near)
    to_far, to_next = (keep[0] + got_far[0]).astype(BF16), (keep[1] + got_far[1]).astype(BF16)
    far = move(to_far, "y", 2)
    next_one = move(to_next, "y", 1)
    to_last = (keep_near[0] + got_near[0]).astype(BF16)
    last_one = move(to_last, "y", 3)
    gamma = keep_near[1] + got_near[1]
    gamma = gamma + next_one.astype(F32) + last_one.astype(F32) + far.astype(F32)
    gamma_out = gamma.reshape(rows, orbitals, v)

    for bits in (3, 1):
        mine, sent = jnp.split(own, 2)
        got = swap_bits(sent, "y", bits)
        own = mine + got
    for axis in ("x", "z"):
        for bits in (1, 3):
            got = swap_bits(own, axis, bits)
            own = own + got
    own = own / task_iblock.shape[0]
    for bits in (1, 3):
        got = swap_bits(own, "y", bits)
        own = jnp.concatenate([own, got])
    got = swap(own)
    density = pl.pallas_call(
        place_kernel,
        in_specs=[SMEM, vmem, vmem],
        out_specs=vmem,
        out_shape=jax.ShapeDtypeStruct((v, v), F32),
        compiler_params=pltpu.CompilerParams(vmem_limit_bytes=4 * 2**20),
        name="place",
    )(place, own, got)
    return gamma_out, density


def solution(mesh):
    finer = Mesh(mesh.devices.reshape(4, 4, 4, 2), AXES)
    placed = (P(OCOL, OROW, None), P(), P(), P(), P(), P())
    return jax.shard_map(
        local, mesh=finer, in_specs=placed, out_specs=(P(OCOL, OROW, None), P()), check_vma=False
    )
```

```python
import jax
import jax.numpy as jnp
from jax import lax
from jax.experimental import pallas as pl
from jax.experimental.pallas import tpu as pltpu
from jax.sharding import Mesh
from jax.sharding import PartitionSpec as P


AXES = ("z", "x", "y", "c")
OROW = ("z", "x")
OCOL = ("y", "c")
BF16 = jnp.bfloat16
F32 = jnp.float32
ANY = pl.BlockSpec(memory_space=pl.ANY)
SMEM = pl.BlockSpec(memory_space=pltpu.SMEM)


def move(x, axis, s):
    n = lax.axis_size(axis)
    return lax.ppermute(x, axis, [(i, (i + s) % n) for i in range(n)])


def swap(x):
    return lax.ppermute(x, "c", [(0, 1), (1, 0)])


def to_plane(turn):
    pairs = []
    for z in range(4):
        for x in range(4):
            for y in range(4):
                for c in range(2):
                    source = ((z * 4 + x) * 4 + y) * 2 + c
                    target = (((2 * (z // 2) + c) * 4 + (x + turn * y) % 4) * 4 + x) * 2 + z % 2
                    pairs.append((source, target))
    return pairs


def turn_kernel(slot_ref, *refs):
    pieces, out_ref, held, sem = refs[:8], refs[8], refs[9], refs[10]
    rows = pieces[0].shape[1]
    copies = [
        pltpu.make_async_copy(
            piece, held.at[:, pl.ds(pl.multiple_of(slot_ref[n] * rows, rows), rows), :], sem.at[n]
        )
        for n, piece in enumerate(pieces)
    ]
    for copy in copies:
        copy.start()
    for copy in copies:
        copy.wait()
    v = held.shape[2]
    for i in range(2):
        out_ref[i * v : (i + 1) * v, :] = held[i].T


def pair_kernel(place_ref, scal_ref, left_ref, row_ref, col_ref, *refs):
    sets_a, sets_b = refs[0:5], refs[5:10]
    parts = (refs[10:12], refs[12:14])
    dens_keep, dens_give = refs[14:16]
    held, k_ref, amp_ref, ampt_ref, dens_ref, both_ref, sem, out_sem = refs[16:]
    rows, v = sets_a[0].shape[1:]

    def at(sets, s, t):
        return sets[s].at[t] if s != 2 else sets[2 if t < 2 else 4].at[t % 2]

    def piece(source, slot, h, half):
        at = pl.ds(pl.multiple_of(slot * rows, rows), rows)
        return pltpu.make_async_copy(
            source, held.at[h, at, half * v : (half + 1) * v], sem.at[h]
        )

    for s in range(4):
        for t in range(4):
            for source, zs, ys, half in (
                (at(sets_a, s, t), s, 4 + t, 0),
                (at(sets_b, s, t), t, 8 + s, 1),
            ):
                zz = place_ref[zs]
                piece(source, 2 * place_ref[ys] + lax.rem(zz, 2), zz // 2, half).start()
    width = 2 * v

    def product(h, step):
        part = slice(step * width // 4, (step + 1) * width // 4)
        k_ref[h, part, :] = jnp.dot(left_ref[part, :], held[h], preferred_element_type=F32)

    def amplitude(h, step):
        i, j = divmod(step, 2)
        a, b = slice(i * v, (i + 1) * v), slice(j * v, (j + 1) * v)
        k = k_ref[h, a, b]
        kt = k.T
        pair = scal_ref[i] + scal_ref[2 + 2 * h + j]
        both = scal_ref[10 + i] * scal_ref[12 + 2 * h + j]
        delta = (pair - col_ref[...]) - row_ref[...]
        amp_ref[a, b] = (both * ((2.0 * k - kt) / delta)).astype(BF16)
        ampt_ref[h, b, a] = (both * ((2.0 * kt - k) / delta)).astype(BF16)

    def density(h):
        part = None
        for i in range(2):
            a = slice(i * v, (i + 1) * v)
            prod = jnp.dot(amp_ref[a, :], ampt_ref[h, :, a], preferred_element_type=F32)
            part = prod if part is None else part + prod
        part = scal_ref[6 + h] * part
        if h == 0:
            dens_ref[...] = part
        else:
            dens_ref[...] += part

    def gamma(h, n):
        at = pl.ds(pl.multiple_of(place_ref[20 + n] * rows, rows), 2 * rows)
        part = scal_ref[8 + h] * jnp.dot(held[h, at, :], ampt_ref[h], preferred_element_type=F32)
        if h == 0:
            both_ref[n] = part
        else:
            both_ref[n] += part

    def leave(n, side):
        core = place_ref[24] if side == 0 else 1 - place_ref[24]
        return pltpu.make_async_copy(
            both_ref.at[n, pl.ds(pl.multiple_of(core * rows, rows), rows), :],
            parts[n // 2][side].at[n % 2],
            out_sem.at[n, side],
        )

    for h in range(2):
        for _ in range(16):
            piece(sets_a[0].at[0], 0, h, 0).wait()
        if h == 0:
            for step in range(4):
                product(0, step)
    for step in range(4):
        product(1, step)
        amplitude(0, step)
    density(0)
    for step in range(4):
        gamma(0, step)
        amplitude(1, step)
    density(1)
    for n in range(4):
        gamma(1, n)
        leave(n, 1).start()
        leave(n, 0).start()
    chunk = v // 8
    for n in range(8):
        start = pl.multiple_of(place_ref[12 + n] * chunk, 8)
        out_ref = dens_keep if n < 4 else dens_give
        out_ref[(n % 4) * chunk : (n % 4 + 1) * chunk, :] = dens_ref[pl.ds(start, chunk), :]
    for n in range(4):
        leave(n, 1).wait()
        leave(n, 0).wait()


def place_kernel(place_ref, mine_ref, other_ref, out_ref):
    chunk = out_ref.shape[0] // 8
    for n in range(8):
        ref = mine_ref if n < 4 else other_ref
        start = pl.multiple_of(place_ref[12 + n] * chunk, 8)
        out_ref[pl.ds(start, chunk), :] = ref[(n % 4) * chunk : (n % 4 + 1) * chunk, :]


def swap_bits(x, axis, bits):
    return lax.ppermute(x, axis, [(i, i ^ bits) for i in range(lax.axis_size(axis))])


def local(integrals, occ_count, occ_energy, vir_energy, task_iblock, task_jblock):
    rows, orbitals, v = integrals.shape
    z, x, y, c = (lax.axis_index(a) for a in AXES)
    my_row = z * 4 + x
    steps = jnp.arange(4)
    shard = jnp.swapaxes(integrals, 0, 1)

    plane_a = lax.ppermute(shard[0], AXES, to_plane(1))
    plane_b = lax.ppermute(shard[1], AXES, to_plane(-1))
    around = [shard]
    for s in (1, 2, 3):
        around.append(move(shard, "y", s))
    across = []
    for part in around:
        across.append(swap(part))
    sets = []
    for half, near, far in ((plane_a, "x", "z"), (plane_b, "z", "x")):
        first = [half]
        for s in (1, 2, 3):
            first.append(move(half, near, s))
        first = jnp.stack(first)
        sets.append([first])
        for s in (1, 3):
            sets[-1].append(move(first, far, s))
    for (_, left, right), far in zip(sets, "zx"):
        low = move(left[:2], far, 1)
        high = move(right[2:], far, 3)
        sets["zx".index(far)] = [sets["zx".index(far)][0], left, low, right, high]
    sets_a, sets_b = sets

    ys = (y - steps) % 4
    slots = jnp.concatenate([2 * ys + c, 2 * ys + 1 - c]).astype(jnp.int32)
    chunks = y ^ jnp.array([0, 1, 3, 2])
    place = jnp.concatenate(
        [
            (z - steps) % 4,
            (x - steps - y) % 4,
            (y - x + steps) % 4,
            4 * c + chunks,
            4 - 4 * c + chunks,
            2 * ((y + jnp.array([2, 1, 3, 0])) % 4),
            c[None],
        ]
    ).astype(jnp.int32)
    blocks = 4 * (2 * jnp.arange(2) + c) + y
    first, second = task_iblock[:, 0], task_jblock
    ours = ((first == my_row)[:, None] & (second[:, None] == blocks[None])).sum(0)
    theirs = ((second == my_row)[:, None] & (first[:, None] == blocks[None])).sum(0)
    energy = occ_energy.reshape(-1, orbitals)
    used = jnp.arange(orbitals)[None, :] < occ_count[:, None]
    scal = jnp.concatenate(
        [
            energy[my_row],
            energy[blocks].reshape(-1),
            ours.astype(F32),
            (ours + theirs).astype(F32),
            used[my_row].astype(F32),
            used[blocks].reshape(-1).astype(F32),
        ]
    )

    vmem = pl.BlockSpec(memory_space=pltpu.VMEM)
    left = pl.pallas_call(
        turn_kernel,
        in_specs=[SMEM] + [ANY] * 8,
        out_specs=vmem,
        out_shape=jax.ShapeDtypeStruct((2 * v, 8 * rows), BF16),
        scratch_shapes=[pltpu.VMEM((2, 8 * rows, v), BF16), pltpu.SemaphoreType.DMA((8,))],
        compiler_params=pltpu.CompilerParams(vmem_limit_bytes=24 * 2**20),
        cost_estimate=pl.CostEstimate(flops=0, bytes_accessed=7_000_000, transcendentals=0),
        name="turn",
    )(slots, *around, *across)

    part = jax.ShapeDtypeStruct((2, rows, 2 * v), F32)
    half = jax.ShapeDtypeStruct((v // 2, v), F32)
    keep, give, keep_near, give_near, dens_keep, dens_give = pl.pallas_call(
        pair_kernel,
        in_specs=[SMEM, SMEM, vmem, vmem, vmem] + [ANY] * 10,
        out_specs=[ANY] * 4 + [vmem] * 2,
        out_shape=[part] * 4 + [half] * 2,
        scratch_shapes=[
            pltpu.VMEM((2, 8 * rows, 2 * v), BF16),
            pltpu.VMEM((2, 2 * v, 2 * v), F32),
            pltpu.VMEM((2 * v, 2 * v), BF16),
            pltpu.VMEM((2, 2 * v, 2 * v), BF16),
            pltpu.VMEM((v, v), F32),
            pltpu.VMEM((4, 2 * rows, 2 * v), F32),
            pltpu.SemaphoreType.DMA((2,)),
            pltpu.SemaphoreType.DMA((4, 2)),
        ],
        compiler_params=pltpu.CompilerParams(vmem_limit_bytes=36 * 2**20),
        cost_estimate=pl.CostEstimate(
            flops=11_800_000_000, bytes_accessed=18_000_000, transcendentals=0
        ),
        name="pairs",
    )(place, scal, left, vir_energy.reshape(1, -1), vir_energy.reshape(-1, 1), *sets_a, *sets_b)

    got = swap(dens_give)
    own = dens_keep + got
    got_far = swap(give)
    got_near = swap(give_near)
    to_far, to_next = (keep[0] + got_far[0]).astype(BF16), (keep[1] + got_far[1]).astype(BF16)
    far = move(to_far, "y", 2)
    next_one = move(to_next, "y", 1)
    to_last = (keep_near[0] + got_near[0]).astype(BF16)
    last_one = move(to_last, "y", 3)
    gamma = keep_near[1] + got_near[1]
    gamma = gamma + next_one.astype(F32) + last_one.astype(F32) + far.astype(F32)
    gamma_out = gamma.reshape(rows, orbitals, v)

    for bits in (3, 1):
        mine, sent = jnp.split(own, 2)
        got = swap_bits(sent, "y", bits)
        own = mine + got
    for axis in ("x", "z"):
        for bits in (1, 3):
            got = swap_bits(own, axis, bits)
            own = own + got
    own = own / task_iblock.shape[0]
    for bits in (1, 3):
        got = swap_bits(own, "y", bits)
        own = jnp.concatenate([own, got])
    got = swap(own)
    density = pl.pallas_call(
        place_kernel,
        in_specs=[SMEM, vmem, vmem],
        out_specs=vmem,
        out_shape=jax.ShapeDtypeStruct((v, v), F32),
        compiler_params=pltpu.CompilerParams(vmem_limit_bytes=4 * 2**20),
        name="place",
    )(place, own, got)
    return gamma_out, density


def solution(mesh):
    finer = Mesh(mesh.devices.reshape(4, 4, 4, 2), AXES)
    placed = (P(OCOL, OROW, None), P(), P(), P(), P(), P())
    return jax.shard_map(
        local, mesh=finer, in_specs=placed, out_specs=(P(OCOL, OROW, None), P()), check_vma=False
    )
```

```python
import jax
import jax.numpy as jnp
from jax import lax
from jax.experimental import pallas as pl
from jax.experimental.pallas import tpu as pltpu
from jax.sharding import Mesh
from jax.sharding import PartitionSpec as P


AXES = ("z", "x", "y", "c")
OROW = ("z", "x")
OCOL = ("y", "c")
BF16 = jnp.bfloat16
F32 = jnp.float32
ANY = pl.BlockSpec(memory_space=pl.ANY)
SMEM = pl.BlockSpec(memory_space=pltpu.SMEM)


def move(x, axis, s):
    n = lax.axis_size(axis)
    return lax.ppermute(x, axis, [(i, (i + s) % n) for i in range(n)])


def swap(x):
    return lax.ppermute(x, "c", [(0, 1), (1, 0)])


def to_plane(turn):
    pairs = []
    for z in range(4):
        for x in range(4):
            for y in range(4):
                for c in range(2):
                    source = ((z * 4 + x) * 4 + y) * 2 + c
                    target = (((2 * (z // 2) + c) * 4 + (x + turn * y) % 4) * 4 + x) * 2 + z % 2
                    pairs.append((source, target))
    return pairs


def turn_kernel(slot_ref, *refs):
    pieces, out_ref, held, sem = refs[:8], refs[8], refs[9], refs[10]
    rows = pieces[0].shape[1]
    copies = [
        pltpu.make_async_copy(
            piece, held.at[:, pl.ds(pl.multiple_of(slot_ref[n] * rows, rows), rows), :], sem.at[n]
        )
        for n, piece in enumerate(pieces)
    ]
    for copy in copies:
        copy.start()
    for copy in copies:
        copy.wait()
    v = held.shape[2]
    for i in range(2):
        out_ref[i * v : (i + 1) * v, :] = held[i].T


def pair_kernel(place_ref, scal_ref, left_ref, row_ref, col_ref, *refs):
    sets_a, sets_b = refs[0:8], refs[8:16]
    parts = (refs[16:18], refs[18:20])
    dens_keep, dens_give = refs[20:22]
    held, k_ref, amp_ref, ampt_ref, dens_ref, both_ref, sem, out_sem = refs[22:]
    rows, v = sets_a[0].shape[1:]

    def at(sets, s, t):
        return sets[2 * s + t // 2].at[t % 2]

    def piece(source, slot, h, half):
        at = pl.ds(pl.multiple_of(slot * rows, rows), rows)
        return pltpu.make_async_copy(
            source, held.at[h, at, half * v : (half + 1) * v], sem.at[h]
        )

    for h in range(2):
        for n in range(4):
            zz = place_ref[n]

            @pl.when(zz // 2 == h)
            def _():
                for m in range(4):
                    for source, ys, half in (
                        (at(sets_a, n, m), 4 + m, 0),
                        (at(sets_b, m, n), 8 + m, 1),
                    ):
                        slot = 2 * place_ref[ys] + lax.rem(zz, 2)
                        piece(source, slot, h, half).start()

    width = 2 * v

    def product(h, step):
        part = slice(step * width // 4, (step + 1) * width // 4)
        k_ref[h, part, :] = jnp.dot(left_ref[part, :], held[h], preferred_element_type=F32)

    def amplitude(h, step):
        i, j = divmod(step, 2)
        a, b = slice(i * v, (i + 1) * v), slice(j * v, (j + 1) * v)
        k = k_ref[h, a, b]
        kt = k.T
        pair = scal_ref[i] + scal_ref[2 + 2 * h + j]
        both = scal_ref[10 + i] * scal_ref[12 + 2 * h + j]
        delta = (pair - col_ref[...]) - row_ref[...]
        amp_ref[a, b] = (both * ((2.0 * k - kt) / delta)).astype(BF16)
        ampt_ref[h, b, a] = (both * ((2.0 * kt - k) / delta)).astype(BF16)

    def density(h):
        part = None
        for i in range(2):
            a = slice(i * v, (i + 1) * v)
            prod = jnp.dot(amp_ref[a, :], ampt_ref[h, :, a], preferred_element_type=F32)
            part = prod if part is None else part + prod
        part = scal_ref[6 + h] * part
        if h == 0:
            dens_ref[...] = part
        else:
            dens_ref[...] += part

    def gamma(h, n):
        at = pl.ds(pl.multiple_of(place_ref[20 + n] * rows, rows), 2 * rows)
        part = scal_ref[8 + h] * jnp.dot(held[h, at, :], ampt_ref[h], preferred_element_type=F32)
        if h == 0:
            both_ref[n] = part
        else:
            both_ref[n] += part

    def leave(n, side):
        core = place_ref[24] if side == 0 else 1 - place_ref[24]
        return pltpu.make_async_copy(
            both_ref.at[n, pl.ds(pl.multiple_of(core * rows, rows), rows), :],
            parts[n // 2][side].at[n % 2],
            out_sem.at[n, side],
        )

    for h in range(2):
        for _ in range(16):
            piece(sets_a[0].at[0], 0, h, 0).wait()
        if h == 0:
            for step in range(4):
                product(0, step)
    for step in range(4):
        product(1, step)
        amplitude(0, step)
    density(0)
    for step in range(4):
        gamma(0, step)
        amplitude(1, step)
    density(1)
    for n in range(4):
        gamma(1, n)
        leave(n, 1).start()
        leave(n, 0).start()
    chunk = v // 8
    for n in range(8):
        start = pl.multiple_of(place_ref[12 + n] * chunk, 8)
        out_ref = dens_keep if n < 4 else dens_give
        out_ref[(n % 4) * chunk : (n % 4 + 1) * chunk, :] = dens_ref[pl.ds(start, chunk), :]
    for n in range(4):
        leave(n, 1).wait()
        leave(n, 0).wait()


def place_kernel(place_ref, *refs):
    *parts, out_ref = refs
    chunk = out_ref.shape[0] // 8
    for n in range(8):
        start = pl.multiple_of(place_ref[12 + n] * chunk, 8)
        out_ref[pl.ds(start, chunk), :] = parts[n][...]


def swap_bits(x, axis, bits):
    return lax.ppermute(x, axis, [(i, i ^ bits) for i in range(lax.axis_size(axis))])


def local(integrals, occ_count, occ_energy, vir_energy, task_iblock, task_jblock):
    rows, orbitals, v = integrals.shape
    z, x, y, c = (lax.axis_index(a) for a in AXES)
    my_row = z * 4 + x
    steps = jnp.arange(4)
    shard = jnp.swapaxes(integrals, 0, 1)

    plane_a = lax.ppermute(shard[0], AXES, to_plane(1))
    plane_b = lax.ppermute(shard[1], AXES, to_plane(-1))
    around = [shard]
    for s in (1, 2, 3):
        around.append(move(shard, "y", s))
    across = []
    for part in around:
        across.append(swap(part))
    sets = []
    for half, near, far in ((plane_a, "x", "z"), (plane_b, "z", "x")):
        first = [half]
        for s in (1, 2, 3):
            first.append(move(half, near, s))
        low, high = jnp.stack(first[:2]), jnp.stack(first[2:])

        def sent(half, s):
            return move(half, far, s)

        low_left = sent(low, 1)
        high_right = sent(high, 3)
        high_left = sent(high, 1)
        low_right = sent(low, 3)
        low_far = sent(low_left, 1)
        high_far = sent(high_right, 3)
        sets.append([low, high, low_left, high_left, low_far, high_far, low_right, high_right])
    sets_a, sets_b = sets

    ys = (y - steps) % 4
    slots = jnp.concatenate([2 * ys + c, 2 * ys + 1 - c]).astype(jnp.int32)
    chunks = y ^ jnp.array([0, 1, 3, 2])
    place = jnp.concatenate(
        [
            (z - steps) % 4,
            (x - steps - y) % 4,
            (y - x + steps) % 4,
            4 * c + chunks,
            4 - 4 * c + chunks,
            2 * ((y + jnp.array([2, 1, 3, 0])) % 4),
            c[None],
        ]
    ).astype(jnp.int32)
    blocks = 4 * (2 * jnp.arange(2) + c) + y
    first, second = task_iblock[:, 0], task_jblock
    ours = ((first == my_row)[:, None] & (second[:, None] == blocks[None])).sum(0)
    theirs = ((second == my_row)[:, None] & (first[:, None] == blocks[None])).sum(0)
    energy = occ_energy.reshape(-1, orbitals)
    used = jnp.arange(orbitals)[None, :] < occ_count[:, None]
    scal = jnp.concatenate(
        [
            energy[my_row],
            energy[blocks].reshape(-1),
            ours.astype(F32),
            (ours + theirs).astype(F32),
            used[my_row].astype(F32),
            used[blocks].reshape(-1).astype(F32),
        ]
    )

    vmem = pl.BlockSpec(memory_space=pltpu.VMEM)
    left = pl.pallas_call(
        turn_kernel,
        in_specs=[SMEM] + [ANY] * 8,
        out_specs=vmem,
        out_shape=jax.ShapeDtypeStruct((2 * v, 8 * rows), BF16),
        scratch_shapes=[pltpu.VMEM((2, 8 * rows, v), BF16), pltpu.SemaphoreType.DMA((8,))],
        compiler_params=pltpu.CompilerParams(vmem_limit_bytes=24 * 2**20),
        cost_estimate=pl.CostEstimate(flops=0, bytes_accessed=7_000_000, transcendentals=0),
        name="turn",
    )(slots, *around, *across)

    part = jax.ShapeDtypeStruct((2, rows, 2 * v), F32)
    half = jax.ShapeDtypeStruct((v // 2, v), F32)
    keep, give, keep_near, give_near, dens_keep, dens_give = pl.pallas_call(
        pair_kernel,
        in_specs=[SMEM, SMEM, vmem, vmem, vmem] + [ANY] * 16,
        out_specs=[ANY] * 4 + [vmem] * 2,
        out_shape=[part] * 4 + [half] * 2,
        scratch_shapes=[
            pltpu.VMEM((2, 8 * rows, 2 * v), BF16),
            pltpu.VMEM((2, 2 * v, 2 * v), F32),
            pltpu.VMEM((2 * v, 2 * v), BF16),
            pltpu.VMEM((2, 2 * v, 2 * v), BF16),
            pltpu.VMEM((v, v), F32),
            pltpu.VMEM((4, 2 * rows, 2 * v), F32),
            pltpu.SemaphoreType.DMA((2,)),
            pltpu.SemaphoreType.DMA((4, 2)),
        ],
        compiler_params=pltpu.CompilerParams(vmem_limit_bytes=36 * 2**20),
        cost_estimate=pl.CostEstimate(
            flops=11_800_000_000, bytes_accessed=18_000_000, transcendentals=0
        ),
        name="pairs",
    )(place, scal, left, vir_energy.reshape(1, -1), vir_energy.reshape(-1, 1), *sets_a, *sets_b)

    got = swap(dens_give)
    own = dens_keep + got
    got_far = swap(give)
    got_near = swap(give_near)
    to_far, to_next = (keep[0] + got_far[0]).astype(BF16), (keep[1] + got_far[1]).astype(BF16)
    far = move(to_far, "y", 2)
    next_one = move(to_next, "y", 1)
    to_last = (keep_near[0] + got_near[0]).astype(BF16)
    last_one = move(to_last, "y", 3)
    gamma = keep_near[1] + got_near[1]
    gamma = gamma + next_one.astype(F32) + last_one.astype(F32) + far.astype(F32)
    gamma_out = gamma.reshape(rows, orbitals, v)

    mine, *others = jnp.split(own, 4)
    others = dict(zip((1, 3, 2), others))
    for bits in (2, 3, 1):
        others[bits] = swap_bits(others[bits], "y", bits)
    own = (mine + others[1]) + (others[2] + others[3])
    for axis in ("x", "z"):
        for bits in (1, 3):
            got = swap_bits(own, axis, bits)
            own = own + got
    own = own / task_iblock.shape[0]
    chunks_of = [own]
    for bits in (2, 3, 1):
        chunks_of.insert(1, swap_bits(own, "y", bits))
    parts = chunks_of + [swap(part) for part in chunks_of]
    density = pl.pallas_call(
        place_kernel,
        in_specs=[SMEM] + [vmem] * 8,
        out_specs=vmem,
        out_shape=jax.ShapeDtypeStruct((v, v), F32),
        compiler_params=pltpu.CompilerParams(vmem_limit_bytes=4 * 2**20),
        name="place",
    )(place, *parts)
    return gamma_out, density


def solution(mesh):
    finer = Mesh(mesh.devices.reshape(4, 4, 4, 2), AXES)
    placed = (P(OCOL, OROW, None), P(), P(), P(), P(), P())
    return jax.shard_map(
        local, mesh=finer, in_specs=placed, out_specs=(P(OCOL, OROW, None), P()), check_vma=False
    )
```

```python
import jax
import jax.numpy as jnp
from jax import lax
from jax.experimental import pallas as pl
from jax.experimental.pallas import tpu as pltpu
from jax.sharding import Mesh
from jax.sharding import PartitionSpec as P


AXES = ("z", "x", "y", "c")
OROW = ("z", "x")
OCOL = ("y", "c")
BF16 = jnp.bfloat16
F32 = jnp.float32
ANY = pl.BlockSpec(memory_space=pl.ANY)
SMEM = pl.BlockSpec(memory_space=pltpu.SMEM)


def move(x, axis, s):
    n = lax.axis_size(axis)
    return lax.ppermute(x, axis, [(i, (i + s) % n) for i in range(n)])


def swap(x):
    return lax.ppermute(x, "c", [(0, 1), (1, 0)])


def to_plane(turn):
    pairs = []
    for z in range(4):
        for x in range(4):
            for y in range(4):
                for c in range(2):
                    source = ((z * 4 + x) * 4 + y) * 2 + c
                    target = (((2 * (z // 2) + c) * 4 + (x + turn * y) % 4) * 4 + x) * 2 + z % 2
                    pairs.append((source, target))
    return pairs


def turn_kernel(slot_ref, *refs):
    pieces, out_ref, held, sem = refs[:8], refs[8], refs[9], refs[10]
    rows = pieces[0].shape[1]
    copies = [
        pltpu.make_async_copy(
            piece, held.at[:, pl.ds(pl.multiple_of(slot_ref[n] * rows, rows), rows), :], sem.at[n]
        )
        for n, piece in enumerate(pieces)
    ]
    for copy in copies:
        copy.start()
    for copy in copies:
        copy.wait()
    v = held.shape[2]
    for i in range(2):
        out_ref[i * v : (i + 1) * v, :] = held[i].T


def pair_kernel(place_ref, scal_ref, left_ref, row_ref, col_ref, *refs):
    sets_a, sets_b = refs[0:8], refs[8:16]
    parts = (refs[16:18], refs[18:20])
    dens_keep, dens_give = refs[20:22]
    held, k_ref, amp_ref, ampt_ref, dens_ref, both_ref, sem, out_sem = refs[22:]
    rows, v = sets_a[0].shape[1:]

    def at(sets, s, t):
        return sets[2 * s + t // 2].at[t % 2]

    def piece(source, slot, h, half):
        at = pl.ds(pl.multiple_of(slot * rows, rows), rows)
        return pltpu.make_async_copy(
            source, held.at[h, at, half * v : (half + 1) * v], sem.at[h]
        )

    for h in range(2):
        for n in range(4):
            zz = place_ref[n]

            @pl.when(zz // 2 == h)
            def _():
                for m in range(4):
                    for source, ys, half in (
                        (at(sets_a, n, m), 4 + m, 0),
                        (at(sets_b, m, n), 8 + m, 1),
                    ):
                        slot = 2 * place_ref[ys] + lax.rem(zz, 2)
                        piece(source, slot, h, half).start()

    width = 2 * v

    def product(h, step):
        part = slice(step * width // 4, (step + 1) * width // 4)
        k_ref[h, part, :] = jnp.dot(left_ref[part, :], held[h], preferred_element_type=F32)

    def amplitude(h, step):
        i, j = divmod(step, 2)
        a, b = slice(i * v, (i + 1) * v), slice(j * v, (j + 1) * v)
        k = k_ref[h, a, b]
        kt = k.T
        pair = scal_ref[i] + scal_ref[2 + 2 * h + j]
        both = scal_ref[10 + i] * scal_ref[12 + 2 * h + j]
        delta = (pair - col_ref[...]) - row_ref[...]
        amp_ref[a, b] = (both * ((2.0 * k - kt) / delta)).astype(BF16)
        ampt_ref[h, b, a] = (both * ((2.0 * kt - k) / delta)).astype(BF16)

    def density(h):
        part = None
        for i in range(2):
            a = slice(i * v, (i + 1) * v)
            prod = jnp.dot(amp_ref[a, :], ampt_ref[h, :, a], preferred_element_type=F32)
            part = prod if part is None else part + prod
        part = scal_ref[6 + h] * part
        if h == 0:
            dens_ref[...] = part
        else:
            dens_ref[...] += part

    def gamma(h, n):
        at = pl.ds(pl.multiple_of(place_ref[20 + n] * rows, rows), 2 * rows)
        part = scal_ref[8 + h] * jnp.dot(held[h, at, :], ampt_ref[h], preferred_element_type=F32)
        if h == 0:
            both_ref[n] = part
        else:
            both_ref[n] += part

    def leave(n, side):
        core = place_ref[24] if side == 0 else 1 - place_ref[24]
        return pltpu.make_async_copy(
            both_ref.at[n, pl.ds(pl.multiple_of(core * rows, rows), rows), :],
            parts[n // 2][side].at[n % 2],
            out_sem.at[n, side],
        )

    for h in range(2):
        for _ in range(16):
            piece(sets_a[0].at[0], 0, h, 0).wait()
        if h == 0:
            for step in range(4):
                product(0, step)
    for step in range(4):
        product(1, step)
        amplitude(0, step)
    density(0)
    for step in range(4):
        gamma(0, step)
        amplitude(1, step)
    density(1)
    for n in range(4):
        gamma(1, n)
        leave(n, 1).start()
        leave(n, 0).start()
    chunk = v // 8
    for n in range(8):
        start = pl.multiple_of(place_ref[12 + n] * chunk, 8)
        out_ref = dens_keep if n < 4 else dens_give
        out_ref[(n % 4) * chunk : (n % 4 + 1) * chunk, :] = dens_ref[pl.ds(start, chunk), :]
    for n in range(4):
        leave(n, 1).wait()
        leave(n, 0).wait()


def place_kernel(place_ref, *refs):
    *parts, out_ref = refs
    chunk = out_ref.shape[0] // 8
    for n in range(8):
        start = pl.multiple_of(place_ref[12 + n] * chunk, 8)
        out_ref[pl.ds(start, chunk), :] = parts[n][...]


def swap_bits(x, axis, bits):
    return lax.ppermute(x, axis, [(i, i ^ bits) for i in range(lax.axis_size(axis))])


def local(integrals, occ_count, occ_energy, vir_energy, task_iblock, task_jblock):
    rows, orbitals, v = integrals.shape
    z, x, y, c = (lax.axis_index(a) for a in AXES)
    my_row = z * 4 + x
    steps = jnp.arange(4)
    shard = jnp.swapaxes(integrals, 0, 1)

    plane_a = lax.ppermute(shard[0], AXES, to_plane(1))
    plane_b = lax.ppermute(shard[1], AXES, to_plane(-1))
    around = [shard]
    for s in (1, 2, 3):
        around.append(move(shard, "y", s))
    across = []
    for part in around:
        across.append(swap(part))
    sets = []
    for half, near, far in ((plane_a, "x", "z"), (plane_b, "z", "x")):
        first = [half]
        for s in (1, 2, 3):
            first.append(move(half, near, s))
        low, high = jnp.stack(first[:2]), jnp.stack(first[2:])

        def sent(half, s):
            return move(half, far, s)

        low_left = sent(low, 1)
        high_right = sent(high, 3)
        high_left = sent(high, 1)
        low_right = sent(low, 3)
        low_far = sent(low_left, 1)
        high_far = sent(high_right, 3)
        sets.append([low, high, low_left, high_left, low_far, high_far, low_right, high_right])
    sets_a, sets_b = sets

    ys = (y - steps) % 4
    slots = jnp.concatenate([2 * ys + c, 2 * ys + 1 - c]).astype(jnp.int32)
    chunks = y ^ jnp.array([0, 1, 3, 2])
    place = jnp.concatenate(
        [
            (z - steps) % 4,
            (x - steps - y) % 4,
            (y - x + steps) % 4,
            4 * c + chunks,
            4 - 4 * c + chunks,
            2 * ((y + jnp.array([2, 1, 3, 0])) % 4),
            c[None],
        ]
    ).astype(jnp.int32)
    blocks = 4 * (2 * jnp.arange(2) + c) + y
    first, second = task_iblock[:, 0], task_jblock
    ours = ((first == my_row)[:, None] & (second[:, None] == blocks[None])).sum(0)
    theirs = ((second == my_row)[:, None] & (first[:, None] == blocks[None])).sum(0)
    energy = occ_energy.reshape(-1, orbitals)
    used = jnp.arange(orbitals)[None, :] < occ_count[:, None]
    scal = jnp.concatenate(
        [
            energy[my_row],
            energy[blocks].reshape(-1),
            ours.astype(F32),
            (ours + theirs).astype(F32),
            used[my_row].astype(F32),
            used[blocks].reshape(-1).astype(F32),
        ]
    )

    vmem = pl.BlockSpec(memory_space=pltpu.VMEM)
    left = pl.pallas_call(
        turn_kernel,
        in_specs=[SMEM] + [ANY] * 8,
        out_specs=vmem,
        out_shape=jax.ShapeDtypeStruct((2 * v, 8 * rows), BF16),
        scratch_shapes=[pltpu.VMEM((2, 8 * rows, v), BF16), pltpu.SemaphoreType.DMA((8,))],
        compiler_params=pltpu.CompilerParams(vmem_limit_bytes=24 * 2**20),
        cost_estimate=pl.CostEstimate(flops=0, bytes_accessed=7_000_000, transcendentals=0),
        name="turn",
    )(slots, *around, *across)

    part = jax.ShapeDtypeStruct((2, rows, 2 * v), F32)
    half = jax.ShapeDtypeStruct((v // 2, v), F32)
    keep, give, keep_near, give_near, dens_keep, dens_give = pl.pallas_call(
        pair_kernel,
        in_specs=[SMEM, SMEM, vmem, vmem, vmem] + [ANY] * 16,
        out_specs=[ANY] * 4 + [vmem] * 2,
        out_shape=[part] * 4 + [half] * 2,
        scratch_shapes=[
            pltpu.VMEM((2, 8 * rows, 2 * v), BF16),
            pltpu.VMEM((2, 2 * v, 2 * v), F32),
            pltpu.VMEM((2 * v, 2 * v), BF16),
            pltpu.VMEM((2, 2 * v, 2 * v), BF16),
            pltpu.VMEM((v, v), F32),
            pltpu.VMEM((4, 2 * rows, 2 * v), F32),
            pltpu.SemaphoreType.DMA((2,)),
            pltpu.SemaphoreType.DMA((4, 2)),
        ],
        compiler_params=pltpu.CompilerParams(vmem_limit_bytes=36 * 2**20),
        cost_estimate=pl.CostEstimate(
            flops=11_800_000_000, bytes_accessed=18_000_000, transcendentals=0
        ),
        name="pairs",
    )(place, scal, left, vir_energy.reshape(1, -1), vir_energy.reshape(-1, 1), *sets_a, *sets_b)

    got = swap(dens_give)
    own = dens_keep + got
    got_far = swap(give)
    got_near = swap(give_near)
    to_far, to_next = (keep[0] + got_far[0]).astype(BF16), (keep[1] + got_far[1]).astype(BF16)
    far = move(to_far, "y", 2)
    next_one = move(to_next, "y", 1)
    to_last = (keep_near[0] + got_near[0]).astype(BF16)
    last_one = move(to_last, "y", 3)
    gamma = keep_near[1] + got_near[1]
    gamma = gamma + next_one.astype(F32) + last_one.astype(F32) + far.astype(F32)
    gamma_out = gamma.reshape(rows, orbitals, v)

    mine, *others = jnp.split(own, 4)
    others = dict(zip((1, 3, 2), others))
    for bits in (2, 3, 1):
        others[bits] = swap_bits(others[bits], "y", bits)
    own = (mine + others[1]) + (others[2] + others[3])
    for bits in (1, 3):
        got = swap_bits(own, "x", bits)
        own = own + got
    got = {}
    for bits in (2, 3, 1):
        got[bits] = swap_bits(own, "z", bits)
    own = (own + got[2]) + (got[1] + got[3])
    own = own / task_iblock.shape[0]
    chunks_of = [own]
    for bits in (2, 3, 1):
        chunks_of.insert(1, swap_bits(own, "y", bits))
    parts = chunks_of + [swap(part) for part in chunks_of]
    density = pl.pallas_call(
        place_kernel,
        in_specs=[SMEM] + [vmem] * 8,
        out_specs=vmem,
        out_shape=jax.ShapeDtypeStruct((v, v), F32),
        compiler_params=pltpu.CompilerParams(vmem_limit_bytes=4 * 2**20),
        name="place",
    )(place, *parts)
    return gamma_out, density


def solution(mesh):
    finer = Mesh(mesh.devices.reshape(4, 4, 4, 2), AXES)
    placed = (P(OCOL, OROW, None), P(), P(), P(), P(), P())
    return jax.shard_map(
        local, mesh=finer, in_specs=placed, out_specs=(P(OCOL, OROW, None), P()), check_vma=False
    )
```
